256 devices in a mesh: rep: 2 (over z_hi), dp: 32 (over z_lo, x, core), mp: 4 (over y).
Axes of the slice: x: 4, y: 4, z: 8 (z_hi: 2, z_lo: 4; z = z_hi * 4 + z_lo), core: 2. Of those that a mesh axis runs over, the one named last changes fastest.
Arguments:
- tokens: bfloat16 [24576, 2048], P(('rep', 'dp', 'mp')), may hold values from -6 to 6
- request_ids: int32 [64, 384], P(('rep', 'dp')), may hold values from 0 to 7, never falling along the last dimension, each value on 1 to 192 neighbouring positions
- cache_entries: bfloat16 [32768, 4096], P(('rep', 'dp', 'mp')), may hold values from -250 to 250, as said below
- cached_lengths: int32 [64, 8], replicated, may hold values from 1 to 256, 512 in all within a row
- traded: int32 [32], P('dp'), may hold values from 0 to 1, as said below
- query_weight: bfloat16 [2048, 2048], P(None, 'mp'), may hold values from -0.125 to 0.125
- key_weight: bfloat16 [2048, 2048], P(None, 'mp'), may hold values from -0.125 to 0.125
- value_weight: bfloat16 [2048, 2048], P(None, 'mp'), may hold values from -0.125 to 0.125
- output_weight: bfloat16 [2048, 2048], P('mp'), may hold values from -0.125 to 0.125
- gate_weight: bfloat16 [2048, 8192], P('dp', 'mp'), may hold values from -0.125 to 0.125
- up_weight: bfloat16 [2048, 8192], P('dp', 'mp'), may hold values from -0.125 to 0.125
- down_weight: bfloat16 [2048, 8192], P('dp', 'mp'), may hold values from -0.0625 to 0.0625
Outputs:
- layer_output: bfloat16 [24576, 2048], P(('rep', 'dp', 'mp'))
The draws below stay inside these ranges and needn't reach their ends.
Inputs may be any that keep to these rules, and one draw needn't show every extreme that they name: `request_ids`: each group's row never falls; every request 0 to 7 has 1 to 192 new tokens in each group, some request exactly 192. `cached_lengths`: each row sums to 512; its largest entry is 256. `traded`: exactly 16 entries are 1. `cache_entries`: keys are stored already rotated to their positions; rows of cache group g are g * 512 to (g + 1) * 512 - 1, the requests' prefixes in request order.
All inputs are finite; a program needn't handle non-finite values.
Results may differ from the reference program's by a relative error of at most 0.013.
The reference program's roundings to bfloat16 on the way count: a program that leaves them out, or rounds other values in their place, can miss the bound.
Values may be sent and summed in bfloat16 or wider, within the bound.
A program may use at most 128 MiB of HBM per device.

```python
import math
import jax
import jax.numpy as jnp
import numpy as np
from jax import lax

D = 2048
HEADS = 16
HEAD_DIM = 128
FF = 8192
TOK_GROUP = 384
CACHE = 512
REQS = 8
PAIRS = 32
GROUPS = 64
TOKENS = 24576
CACHE_ROWS = 32768


def draw_cache_entries(key, part):
    rows = CACHE_ROWS
    base = jax.random.normal(jax.random.fold_in(key, 11), (rows, 2 * D), jnp.float32)
    base = jnp.clip(base, -6.0, 6.0)
    return base.astype(jnp.bfloat16)


def draw_traded(key, part):
    order = jax.random.permutation(jax.random.fold_in(key, 21), PAIRS)
    return (order < PAIRS // 2).astype(jnp.int32)


def steps_of(own_key, extent, shards, low, top_value):
    loudness, own = 1.0, jax.random.fold_in(own_key, 6)
    for axis_at, blocks in shards:
        heights = jnp.exp(jax.random.uniform(jax.random.fold_in(own, axis_at), (blocks,), jnp.float32, low / len(shards), top_value / len(shards)))
        loudness = loudness * jnp.repeat(heights, extent[axis_at] // blocks).reshape([-1 if axis == axis_at else 1 for axis in range(len(extent))])
    return loudness


def length_profile(amount, total, reach, lean):
    weights = [(1 << 20) // math.isqrt(standing ** lean) + 1 for standing in range(2, amount + 1)]
    spare, holding = total - reach - (amount - 1), [1] * (amount - 1)
    while spare > 0:
        movable = [i for i in range(amount - 1) if holding[i] < reach]
        pool, budget = sum([weights[i] for i in movable]), spare
        for i in movable:
            more = min(reach - holding[i], max(1, budget * weights[i] // pool), spare)
            holding[i] = holding[i] + more
            spare = spare - more
    return np.array([reach] + holding)


def ragged_sizes(rng, count, total, most, slope):
    if count == 2:
        one = jax.random.randint(rng, (), max(1, total - most), min(most, total - 1) + 1)
        return jnp.stack([one, total - one])
    lengths = jnp.asarray(length_profile(count, total, most, slope), jnp.int32)
    couples = (count - 1) // 2
    giver, receiver = lengths[1:1 + 2 * couples:2], lengths[2:2 + 2 * couples:2]
    slack = jnp.minimum(giver - 1, most - receiver)
    passed = jax.random.randint(jax.random.fold_in(rng, 1), (couples,), 0, 1 << 20) % (slack + 1)
    lengths = lengths.at[1:1 + 2 * couples:2].set(giver - passed).at[2:2 + 2 * couples:2].set(receiver + passed)
    return lengths[jax.random.permutation(jax.random.fold_in(rng, 2), count)]


def noise(rng, extent, scale, reach, pieces=(), kind=jnp.bfloat16):
    drawn = scale * jax.random.normal(rng, extent, jnp.float32)
    if pieces:
        drawn = drawn * steps_of(rng, extent, pieces, -0.22, 0.18)
    return jnp.clip(drawn, -reach, reach).astype(kind)


def setup_inputs(seed: int = 0) -> dict:
    arg_keys = jax.random.split(jax.random.key(seed), 13)
    tokens = noise(arg_keys[0], (TOKENS, D), 1.0, 6.0, ((0, 256),))
    request_ids = jax.vmap(lambda own: jnp.searchsorted(jnp.cumsum(ragged_sizes(own, REQS, TOK_GROUP, TOK_GROUP // 2, 2)), jnp.arange(TOK_GROUP), side="right"))(jax.random.split(arg_keys[1], GROUPS)).reshape((GROUPS, TOK_GROUP)).astype(jnp.int32)
    cache_entries = draw_cache_entries(jax.random.fold_in(arg_keys[12], 71), 0)
    cached_lengths = jax.vmap(lambda own: ragged_sizes(own, REQS, CACHE, CACHE // 2, 2))(jax.random.split(arg_keys[3], GROUPS)).reshape((GROUPS, REQS)).astype(jnp.int32)
    traded = draw_traded(jax.random.fold_in(arg_keys[12], 71), 0)
    query_weight = noise(arg_keys[5], (D, D), D ** -0.5, 0.125, ((1, 4),))
    key_weight = noise(arg_keys[6], (D, D), D ** -0.5, 0.125, ((1, 4),))
    value_weight = noise(arg_keys[7], (D, D), D ** -0.5, 0.125, ((1, 4),))
    output_weight = noise(arg_keys[8], (D, D), D ** -0.5, 0.125, ((0, 4),))
    gate_weight = noise(arg_keys[9], (D, FF), D ** -0.5, 0.125, ((0, 32), (1, 4)))
    up_weight = noise(arg_keys[10], (D, FF), D ** -0.5, 0.125, ((0, 32), (1, 4)))
    down_weight = noise(arg_keys[11], (D, FF), FF ** -0.5, 0.0625, ((0, 32), (1, 4)))
    return dict(tokens=tokens, request_ids=request_ids, cache_entries=cache_entries, cached_lengths=cached_lengths, traded=traded, query_weight=query_weight, key_weight=key_weight, value_weight=value_weight, output_weight=output_weight, gate_weight=gate_weight, up_weight=up_weight, down_weight=down_weight)


EPSILON = 1e-05
ROPE_BASE = 10000.0

def layer_norm(rows):
    center = rows - lax.optimization_barrier(jnp.mean(rows, axis=-1, keepdims=True))
    spread = lax.optimization_barrier(jnp.mean(center * center, axis=-1, keepdims=True))
    return center * lax.rsqrt(spread + EPSILON)

def request_layout(request_row, length_row, cache_size):
    number = length_row.shape[0]
    labels = jnp.arange(number, dtype=jnp.int32)
    onehot = (request_row[:, None] == labels[None, :]).astype(jnp.int32)
    counts = lax.optimization_barrier(jnp.sum(onehot, axis=0))
    starts = jnp.cumsum(counts) - counts
    token_place = jnp.arange(request_row.shape[0], dtype=jnp.int32)
    positions = lax.optimization_barrier(jnp.sum(onehot * (length_row - starts)[None, :], axis=1)) + token_place
    bounds = jnp.cumsum(length_row)
    cache_place = jnp.arange(cache_size, dtype=jnp.int32)
    owner = lax.optimization_barrier(jnp.sum((cache_place[:, None] >= bounds[None, :]).astype(jnp.int32), axis=1))
    return (positions.astype(jnp.int32), owner.astype(jnp.int32))

def rotate(vectors, positions):
    half = vectors.shape[-1] // 2
    freq = ROPE_BASE ** (-jnp.arange(half, dtype=jnp.float32) / half)
    angle = positions.astype(jnp.float32)[:, None] * freq[None, :]
    cosine = jnp.cos(angle)[:, None, :]
    sine = jnp.sin(angle)[:, None, :]
    first = vectors[..., :half]
    second = vectors[..., half:]
    return jnp.concatenate([first * cosine - second * sine, second * cosine + first * sine], axis=-1)

def attend(query, keys_new, values_new, keys_cache, values_cache, request_row, owner):
    scale = 1.0 / math.sqrt(query.shape[-1])
    keys = jnp.concatenate([keys_cache, keys_new], axis=0)
    values = jnp.concatenate([values_cache, values_new], axis=0)
    scores = jnp.einsum('thd,khd->htk', query.astype(jnp.float32), keys.astype(jnp.float32)) * scale
    count = request_row.shape[0]
    place = jnp.arange(count, dtype=jnp.int32)
    same_cache = owner[None, :] == request_row[:, None]
    same_new = (request_row[None, :] == request_row[:, None]) & (place[None, :] <= place[:, None])
    allowed = jnp.concatenate([same_cache, same_new], axis=1)
    scores = jnp.where(allowed[None], scores, -1e+30)
    top = lax.optimization_barrier(jnp.max(scores, axis=-1, keepdims=True))
    raised = jnp.exp(scores - top)
    total = lax.optimization_barrier(jnp.sum(raised, axis=-1, keepdims=True))
    weights = (raised / total).astype(jnp.bfloat16)
    mixed = jnp.einsum('htk,khd->thd', weights.astype(jnp.float32), values.astype(jnp.float32))
    return mixed.astype(jnp.bfloat16)

def reference(tokens, request_ids, cache_entries, cached_lengths, traded, query_weight, key_weight, value_weight, output_weight, gate_weight, up_weight, down_weight):

    def one_group(group):
        replica = group // PAIRS
        within = group % PAIRS
        source = jnp.where(traded[within] == 1, (1 - replica) * PAIRS + within, group).astype(jnp.int32)
        rows = lax.dynamic_slice_in_dim(tokens, (group * TOK_GROUP).astype(jnp.int32), TOK_GROUP, 0)
        request_row = lax.dynamic_slice_in_dim(request_ids, group.astype(jnp.int32), 1, 0)[0]
        length_row = lax.dynamic_slice_in_dim(cached_lengths, source, 1, 0)[0]
        stored = lax.dynamic_slice_in_dim(cache_entries, (source * CACHE).astype(jnp.int32), CACHE, 0)
        positions, owner = request_layout(request_row, length_row, CACHE)
        normed = layer_norm(rows.astype(jnp.float32)).astype(jnp.bfloat16)
        query = jnp.dot(normed, query_weight, preferred_element_type=jnp.float32).reshape(TOK_GROUP, HEADS, HEAD_DIM)
        query = rotate(query, positions).astype(jnp.bfloat16)
        keys_new = jnp.dot(normed, key_weight, preferred_element_type=jnp.float32).reshape(TOK_GROUP, HEADS, HEAD_DIM)
        keys_new = rotate(keys_new, positions).astype(jnp.bfloat16)
        values_new = jnp.dot(normed, value_weight, preferred_element_type=jnp.float32).astype(jnp.bfloat16).reshape(TOK_GROUP, HEADS, HEAD_DIM)
        keys_cache = stored[:, :D].reshape(CACHE, HEADS, HEAD_DIM)
        values_cache = stored[:, D:].reshape(CACHE, HEADS, HEAD_DIM)
        mixed = attend(query, keys_new, values_new, keys_cache, values_cache, request_row, owner)
        attention = jnp.dot(mixed.reshape(TOK_GROUP, D), output_weight, preferred_element_type=jnp.float32)
        state = (rows.astype(jnp.float32) + attention).astype(jnp.bfloat16)
        normed_two = layer_norm(state.astype(jnp.float32)).astype(jnp.bfloat16)
        gate = jnp.dot(normed_two, gate_weight, preferred_element_type=jnp.float32)
        upward = jnp.dot(normed_two, up_weight, preferred_element_type=jnp.float32)
        activated = (jax.nn.silu(gate) * upward).astype(jnp.bfloat16)
        projected = jnp.dot(activated, down_weight.T, preferred_element_type=jnp.float32)
        return (state.astype(jnp.float32) + projected).astype(jnp.bfloat16)
    outputs = lax.map(one_group, jnp.arange(GROUPS, dtype=jnp.int32))
    return outputs.reshape(TOKENS, D)
```

```python
import functools
import math

import jax
import jax.numpy as jnp
import numpy as np
from jax import lax
from jax.experimental import pallas as pl
from jax.experimental.pallas import tpu as pltpu
from jax.sharding import PartitionSpec as P

D = 2048
FF = 2048
HEADS = 4
HEAD_DIM = 128
WIDTH = HEADS * HEAD_DIM
GROUP = 384
OWN = 96
CACHE = 512
REQS = 8
EPSILON = 1e-05
ROPE_BASE = 10000.0
MESH = pl.DeviceIdType.MESH

STREAMS = (
    (0, 0, 64, True),
    (1, 0, 64, False),
    (2, 0, 32, True),
    (2, 32, 64, False),
)
N_STREAM_COPIES = 8
N_SIB_COPIES = 6
TILES = 4
TILE = D // TILES


def normalize(rows):
    center = rows - jnp.mean(rows, axis=-1, keepdims=True)
    spread = jnp.mean(center * center, axis=-1, keepdims=True)
    return center * lax.rsqrt(spread + EPSILON)


def dot(a, b, dims=(((1,), (0,)), ((), ()))):
    return lax.dot_general(a, b, dims, preferred_element_type=jnp.float32)


class Copies:
    def __init__(self, send, recv):
        self.send, self.recv, self.used, self.all = send, recv, 0, []

    def start(self, src, dst, device):
        copy = pltpu.make_async_remote_copy(
            src_ref=src,
            dst_ref=dst,
            send_sem=self.send.at[self.used],
            recv_sem=self.recv.at[self.used],
            device_id=device,
            device_id_type=MESH,
        )
        self.used += 1
        self.all.append(copy)
        copy.start()
        return copy


class Stream:
    def __init__(self, spec, net, w_ref, place, neighbours):
        self.weight, self.first, self.end, self.x_first = spec
        self.mid = (self.first + self.end) // 2
        self.net, self.w = net, w_ref
        self.zl, self.x, self.core = place
        xp, xm, zp, zm, self.sibling = neighbours
        self.near = (xp, xm) if self.x_first else (zp, zm)
        self.far = (zp, zm) if self.x_first else (xp, xm)
        self.step = 0
        self.to_sibling = []

    def at(self, near, far, lo, hi):
        x_off, z_off = (near, far) if self.x_first else (far, near)
        x = slice(None) if x_off is None else lax.rem(self.x + x_off + 4, 4)
        zl = slice(None) if z_off is None else lax.rem(self.zl + z_off + 4, 4)
        return self.w.at[self.weight, zl, x, self.core, lo:hi]

    def push(self, part, device):
        return self.net.start(part, part, device)

    def advance(self):
        lo, mid, hi = self.first, self.mid, self.end
        plus, minus = self.near
        up, down = self.far
        if self.step == 0:
            own = self.at(0, 0, lo, hi)
            self.a = (self.push(own, plus), self.push(own, minus))
        elif self.step == 1:
            self.a[0].wait_recv()
            self.a[1].wait_recv()
            self.b = (
                self.push(self.at(-1, 0, lo, mid), plus),
                self.push(self.at(1, 0, mid, hi), minus),
            )
            self.sib(self.at(-1, 0, lo, hi))
            self.sib(self.at(1, 0, lo, hi))
        elif self.step == 2:
            self.b[0].wait_recv()
            self.b[1].wait_recv()
            line = self.at(None, 0, lo, hi)
            self.c = (self.push(line, up), self.push(line, down))
            self.sib(self.at(2, 0, lo, hi))
        elif self.step == 3:
            self.c[0].wait_recv()
            self.c[1].wait_recv()
            self.d = (
                self.push(self.at(None, -1, lo, mid), up),
                self.push(self.at(None, 1, mid, hi), down),
            )
            self.sib(self.at(None, -1, lo, hi))
            self.sib(self.at(None, 1, lo, hi))
        elif self.step == 4:
            self.d[0].wait_recv()
            self.d[1].wait_recv()
            self.sib(self.at(None, 2, lo, hi))
        elif self.step == 5:
            for copy in self.to_sibling:
                copy.wait_recv()
        self.step += 1

    def sib(self, part):
        self.to_sibling.append(self.push(part, self.sibling))


def kernel(
    traded_ref,
    lengths_ref,
    tokens_ref,
    ids_ref,
    freq_ref,
    cache_ref,
    wq_ref,
    wk_ref,
    wv_ref,
    wo_ref,
    gate_ref,
    up_ref,
    down_ref,
    out_ref,
    w,
    qkv_w,
    o_w,
    cache,
    other_tokens,
    other_ids,
    normed,
    query,
    key,
    value,
    cosine,
    sine,
    bias,
    mixed,
    terms,
    send_one,
    recv_one,
    state,
    normed_two,
    hidden,
    send_two,
    recv_two,
    done,
    other_done,
    send_sem,
    recv_sem,
    local_sem,
):
    rep, dp, mp = lax.axis_index("rep"), lax.axis_index("dp"), lax.axis_index("mp")
    zl, x, core = dp // 8, lax.rem(dp // 2, 4), lax.rem(dp, 2)
    z = rep * 4 + zl

    def at_z(where):
        where = lax.rem(where + 8, 8)
        return (where // 4, (lax.rem(where, 4) * 4 + x) * 2 + core, mp)

    def at_x(where):
        return (rep, (zl * 4 + lax.rem(where + 4, 4)) * 2 + core, mp)

    sibling = (rep, (zl * 4 + x) * 2 + (1 - core), mp)
    partner = (1 - rep, dp, mp)
    peers = [(rep, dp, lax.rem(mp + k, 4)) for k in (1, 2, 3)]
    around = (at_x(x + 1), at_x(x - 1), at_z(z + 1), at_z(z - 1), sibling)

    locals_ = []

    def fetch(src, dst):
        copy = pltpu.make_async_copy(src, dst, local_sem.at[len(locals_)])
        locals_.append(copy)
        copy.start()
        return copy

    shards = [
        fetch(ref, w.at[i, zl, x, core]) for i, ref in enumerate((gate_ref, up_ref, down_ref))
    ]

    barrier = pltpu.get_barrier_semaphore()
    friends = peers + [partner] + list(around)
    for friend in friends:
        pl.semaphore_signal(barrier, inc=1, device_id=friend, device_id_type=MESH)
    pl.semaphore_wait(barrier, len(friends))

    net = Copies(send_sem, recv_sem)
    swap_ids = net.start(ids_ref, other_ids, partner)
    swap_in = net.start(tokens_ref, other_tokens, partner)
    for copy in shards:
        copy.wait()
    streams = [Stream(spec, net, w, (zl, x, core), around) for spec in STREAMS]
    for stream in streams:
        stream.advance()
    own_shard = w.at[:, zl, x, core]
    sib_own = net.start(own_shard, own_shard, sibling)
    qkv_copies = [fetch(ref, qkv_w.at[i]) for i, ref in enumerate((wq_ref, wk_ref, wv_ref))]
    o_copy = fetch(wo_ref, o_w)
    cache_rows = pl.ds(pl.multiple_of(mp * 128, 128), 128)
    cache_copies = []
    for k in range(4):
        to = lax.rem(mp + k, 4)
        for i in range(2):
            columns = pl.ds(pl.multiple_of(i * D + to * WIDTH, WIDTH), WIDTH)
            src, dst = cache_ref.at[:, columns], cache.at[i, cache_rows]
            if k == 0:
                cache_copies.append(fetch(src, dst))
            else:
                cache_copies.append(net.start(src, dst, peers[k - 1]))

    moved = traded_ref[0] == 1
    swap_ids.wait_recv()
    swap_in.wait_recv()
    tokens = jnp.where(moved, other_tokens[...], tokens_ref[...])
    own_rows = pl.ds(pl.multiple_of(mp * OWN, OWN), OWN)
    normed[own_rows, :] = normalize(tokens.astype(jnp.float32)).astype(jnp.bfloat16)
    gathers = [net.start(normed.at[own_rows], normed.at[own_rows], peer) for peer in peers]

    group = rep * 32 + dp
    ids = jnp.where(moved, other_ids[...], ids_ref[...])
    place = lax.broadcasted_iota(jnp.int32, (1, GROUP), 1)
    positions = place
    cached_place = lax.broadcasted_iota(jnp.int32, (1, CACHE), 1)
    owner = jnp.zeros((1, CACHE), jnp.int32)
    bound = 0
    for s in range(REQS):
        length = lengths_ref[group, s]
        start = jnp.sum((ids < s).astype(jnp.int32), axis=1, keepdims=True)
        positions = positions + jnp.where(ids == s, length - start, 0)
        bound = bound + length
        owner = owner + (cached_place >= bound).astype(jnp.int32)
    ids_column = jnp.transpose(jnp.broadcast_to(ids.astype(jnp.float32), (128, GROUP)))
    places_column = jnp.transpose(jnp.broadcast_to(positions.astype(jnp.float32), (128, GROUP)))
    angle = places_column * freq_ref[...]
    cosine[...] = jnp.cos(angle)
    lane = lax.broadcasted_iota(jnp.int32, (GROUP, HEAD_DIM), 1)
    wave = jnp.sin(angle)
    sine[...] = jnp.where(lane < HEAD_DIM // 2, -wave, wave)
    column = ids_column[:, :1]
    bias[:, :CACHE] = jnp.where(column == owner.astype(jnp.float32), 0.0, -1e30)
    row_at = lax.broadcasted_iota(jnp.int32, (GROUP, GROUP), 0)
    column_at = lax.broadcasted_iota(jnp.int32, (GROUP, GROUP), 1)
    same = (column == ids.astype(jnp.float32)) & (column_at <= row_at)
    bias[:, CACHE:] = jnp.where(same, 0.0, -1e30)

    for stream in streams:
        stream.advance()
    for copy in gathers:
        copy.wait_recv()
    for copy in qkv_copies:
        copy.wait()
    for stream in streams:
        stream.advance()

    @pl.loop(0, HEADS // 2)
    def _(pair):
        columns = pl.ds(pl.multiple_of(pair * 256, 256), 256)
        rows = normed[...]
        q = dot(rows, qkv_w[0, :, columns])
        k = dot(rows, qkv_w[1, :, columns])
        v = dot(rows, qkv_w[2, :, columns])
        value[:, columns] = v.astype(jnp.bfloat16)
        for source, target in ((q, query), (k, key)):
            for half in range(2):
                head = source[:, half * HEAD_DIM : (half + 1) * HEAD_DIM]
                turned = head * cosine[...] + pltpu.roll(head, HEAD_DIM // 2, 1) * sine[...]
                place_at = pl.ds(
                    pl.multiple_of(pair * 256 + half * HEAD_DIM, HEAD_DIM), HEAD_DIM
                )
                target[:, place_at] = turned.astype(jnp.bfloat16)

    for copy in cache_copies[:2]:
        copy.wait()
    for copy in cache_copies[2:]:
        copy.wait_recv()

    scale = 1.0 / math.sqrt(HEAD_DIM)

    @pl.loop(0, HEADS)
    def _(h):
        columns = pl.ds(pl.multiple_of(h * HEAD_DIM, HEAD_DIM), HEAD_DIM)
        inner = (((1,), (1,)), ((), ()))
        for block in range(3):
            rows = slice(block * 128, block * 128 + 128)
            seen = block * 128 + 128
            q = query[rows, columns]
            old = dot(q, cache[0, :, columns], inner) * scale + bias[rows, :CACHE]
            new = dot(q, key[:seen, columns], inner) * scale + bias[rows, CACHE : CACHE + seen]
            top = jnp.maximum(
                jnp.max(old, axis=1, keepdims=True), jnp.max(new, axis=1, keepdims=True)
            )
            old, new = jnp.exp(old - top), jnp.exp(new - top)
            total = jnp.sum(old, axis=1, keepdims=True) + jnp.sum(new, axis=1, keepdims=True)
            share = 1.0 / total
            out = dot((old * share).astype(jnp.bfloat16), cache[1, :, columns])
            out = out + dot((new * share).astype(jnp.bfloat16), value[:seen, columns])
            mixed[rows, columns] = out.astype(jnp.bfloat16)

    o_copy.wait()

    def scatter(tile, part, send, recv):
        columns = slice(tile * TILE, (tile + 1) * TILE)
        terms[:, columns] = part
        send[:, columns] = part.astype(jnp.bfloat16)
        copies = []
        for k in (1, 2, 3):
            rows = pl.ds(pl.multiple_of(lax.rem(mp + k, 4) * OWN, OWN), OWN)
            copies.append(
                net.start(send.at[rows, columns], recv.at[k - 1, :, columns], peers[k - 1])
            )
        return copies

    def collect(tile, copies, recv):
        columns = slice(tile * TILE, (tile + 1) * TILE)
        for copy in copies:
            copy.wait_recv()
        total = terms[own_rows, columns]
        for k in range(3):
            total = total + recv[k, :, columns].astype(jnp.float32)
        return total

    scattered = []
    for tile in range(TILES):
        part = dot(mixed[...], o_w[:, tile * TILE : (tile + 1) * TILE])
        scattered.append(scatter(tile, part, send_one, recv_one))

    for stream in streams:
        stream.advance()

    for tile in range(TILES):
        columns = slice(tile * TILE, (tile + 1) * TILE)
        own = jnp.where(moved, other_tokens[:, columns], tokens_ref[:, columns])
        total = collect(tile, scattered[tile], recv_one)
        state[:, columns] = (own.astype(jnp.float32) + total).astype(jnp.bfloat16)
    normed_two[own_rows, :] = normalize(state[...].astype(jnp.float32)).astype(jnp.bfloat16)
    gathers = [
        net.start(normed_two.at[own_rows], normed_two.at[own_rows], peer) for peer in peers
    ]

    for stream in streams:
        stream.advance()
    for stream in streams:
        stream.advance()
    sib_own.wait_recv()
    for copy in gathers:
        copy.wait_recv()

    @pl.loop(0, FF // 256)
    def _(tile):
        columns = pl.ds(pl.multiple_of(tile * 256, 256), 256)
        rows = normed_two[...]
        gate = dot(rows, w[0, :, :, :, :, columns].reshape(D, 256))
        upward = dot(rows, w[1, :, :, :, :, columns].reshape(D, 256))
        hidden[:, columns] = (gate / (1.0 + jnp.exp(-gate)) * upward).astype(jnp.bfloat16)

    scattered = []
    for tile in range(TILES):
        part = dot(
            hidden[...], w[2, tile].reshape(TILE, FF), (((1,), (1,)), ((), ()))
        )
        scattered.append(scatter(tile, part, send_two, recv_two))
    returns = []
    for tile in range(TILES):
        columns = slice(tile * TILE, (tile + 1) * TILE)
        total = collect(tile, scattered[tile], recv_two)
        done[:, columns] = (state[:, columns].astype(jnp.float32) + total).astype(jnp.bfloat16)
        returns.append(
            net.start(done.at[:, columns], other_done.at[:, columns], partner)
        )
    for tile in range(TILES):
        columns = slice(tile * TILE, (tile + 1) * TILE)
        returns[tile].wait_recv()
        out_ref[:, columns] = jnp.where(moved, other_done[:, columns], done[:, columns])
    for copy in net.all:
        copy.wait_send()


N_COPIES = 2 + (N_STREAM_COPIES + N_SIB_COPIES) * len(STREAMS) + 1 + 6 + 3 + 3 * TILES + 3 + 3 * TILES + TILES


def local(
    tokens,
    request_ids,
    cache_entries,
    cached_lengths,
    traded,
    query_weight,
    key_weight,
    value_weight,
    output_weight,
    gate_weight,
    up_weight,
    down_weight,
):
    half = HEAD_DIM // 2
    freq = ROPE_BASE ** (-np.arange(half, dtype=np.float64) / half)
    freq = jnp.asarray(np.concatenate([freq, freq])[None].astype(np.float32))
    bf16, f32 = jnp.bfloat16, jnp.float32
    in_vmem = pl.BlockSpec(memory_space=pltpu.VMEM)
    in_smem = pl.BlockSpec(memory_space=pltpu.SMEM)
    in_hbm = pl.BlockSpec(memory_space=pl.ANY)
    return pl.pallas_call(
        kernel,
        out_shape=jax.ShapeDtypeStruct((OWN, D), bf16),
        in_specs=[in_smem, in_smem, in_vmem, in_vmem, in_vmem] + [in_hbm] * 8,
        out_specs=in_vmem,
        scratch_shapes=[
            pltpu.VMEM((3, 4, 4, 2, 64, D), bf16),
            pltpu.VMEM((3, D, WIDTH), bf16),
            pltpu.VMEM((WIDTH, D), bf16),
            pltpu.VMEM((2, CACHE, WIDTH), bf16),
            pltpu.VMEM((OWN, D), bf16),
            pltpu.VMEM((1, GROUP), jnp.int32),
            pltpu.VMEM((GROUP, D), bf16),
            pltpu.VMEM((GROUP, WIDTH), bf16),
            pltpu.VMEM((GROUP, WIDTH), bf16),
            pltpu.VMEM((GROUP, WIDTH), bf16),
            pltpu.VMEM((GROUP, HEAD_DIM), f32),
            pltpu.VMEM((GROUP, HEAD_DIM), f32),
            pltpu.VMEM((GROUP, CACHE + GROUP), f32),
            pltpu.VMEM((GROUP, WIDTH), bf16),
            pltpu.VMEM((GROUP, D), f32),
            pltpu.VMEM((GROUP, D), bf16),
            pltpu.VMEM((3, OWN, D), bf16),
            pltpu.VMEM((OWN, D), bf16),
            pltpu.VMEM((GROUP, D), bf16),
            pltpu.VMEM((GROUP, FF), bf16),
            pltpu.VMEM((GROUP, D), bf16),
            pltpu.VMEM((3, OWN, D), bf16),
            pltpu.VMEM((OWN, D), bf16),
            pltpu.VMEM((OWN, D), bf16),
            pltpu.SemaphoreType.DMA((N_COPIES,)),
            pltpu.SemaphoreType.DMA((N_COPIES,)),
            pltpu.SemaphoreType.DMA((9,)),
        ],
        compiler_params=pltpu.CompilerParams(
            collective_id=0, has_side_effects=True, vmem_limit_bytes=60 * 1024 * 1024
        ),
        name="layer",
    )(
        traded,
        cached_lengths,
        tokens,
        request_ids,
        freq,
        cache_entries,
        query_weight,
        key_weight,
        value_weight,
        output_weight,
        gate_weight,
        up_weight,
        down_weight,
    )


def solution(mesh):
    in_specs = (
        P(("rep", "dp", "mp"), None),
        P(("rep", "dp"), None),
        P(("rep", "dp", "mp"), None),
        P(),
        P("dp"),
        P(None, "mp"),
        P(None, "mp"),
        P(None, "mp"),
        P("mp", None),
        P("dp", "mp"),
        P("dp", "mp"),
        P("dp", "mp"),
    )
    out_specs = P(("rep", "dp", "mp"), None)
    return jax.shard_map(local, mesh=mesh, in_specs=in_specs, out_specs=out_specs, check_vma=False)
```

```python
import functools
import math

import jax
import jax.numpy as jnp
import numpy as np
from jax import lax
from jax.experimental import pallas as pl
from jax.experimental.pallas import tpu as pltpu
from jax.sharding import PartitionSpec as P

D = 2048
FF = 2048
HEADS = 4
HEAD_DIM = 128
WIDTH = HEADS * HEAD_DIM
GROUP = 384
OWN = 96
CACHE = 512
REQS = 8
EPSILON = 1e-05
ROPE_BASE = 10000.0
MESH = pl.DeviceIdType.MESH

STREAMS = ((0, 0, 64, True), (1, 0, 64, False), (2, 0, 64, False))
SIBLING = {"s0": (0, 3), "s1": (3, 5), "s2": (5, 6)}
PLAN = {
    "issue": ("g.start_near", "u.start_far", "g.start_far", "d.start_far",),
    "swap0": (),
    "swap1": ("u.start_near",),
    "swap2": ("g.e1",),
    "ag1": ("g.e2", "u.e3",),
    "qkv": ("u.e1", "g.e3",),
    "attn0": (),
    "attn1": ("u.e2",),
    "rs0": ("u.e4", "d.start_near",),
    "rs1": ("g.e4", "u.e5", "d.e1",),
    "ag2": ("g.e5", "d.e3", "d.e2", "g.e6", "u.e6", "g.e7", "u.e7",),
    "up0": ("d.e4",),
    "up1": ("d.e5",),
    "tile0": ("d.s0",),
    "tile1": ("d.s1", "d.e6",),
    "tile3": ("d.s2",),
}
N_STREAM_COPIES = 26
HALF = GROUP // 2
PART = OWN // 2
CHUNKS = 3
CHUNK = OWN // CHUNKS
LAG = 2
TILE = 512


def normalize(rows):
    center = rows - jnp.mean(rows, axis=-1, keepdims=True)
    spread = jnp.mean(center * center, axis=-1, keepdims=True)
    return center * lax.rsqrt(spread + EPSILON)


def dot(a, b, dims=(((1,), (0,)), ((), ()))):
    return lax.dot_general(a, b, dims, preferred_element_type=jnp.float32)


class Copies:
    def __init__(self, send, recv):
        self.send, self.recv, self.used, self.all, self.gone = send, recv, 0, [], []

    def start(self, src, dst, device):
        copy = pltpu.make_async_remote_copy(
            src_ref=src,
            dst_ref=dst,
            send_sem=self.send.at[self.used],
            recv_sem=self.recv.at[self.used],
            device_id=device,
            device_id_type=MESH,
        )
        self.used += 1
        self.all.append(copy)
        copy.start()
        return copy

    def leave(self, copies):
        for copy in copies:
            copy.wait_send()
            self.gone.append(copy)


class Stream:
    def __init__(self, spec, net, w_ref, place, neighbours):
        self.weight, self.first, self.end, self.x_first = spec
        self.mid = (self.first + self.end) // 2
        self.net, self.w = net, w_ref
        self.zl, self.x, self.core = place
        xp, xm, zp, zm, self.sibling = neighbours
        self.near = (xp, xm) if self.x_first else (zp, zm)
        self.far = (zp, zm) if self.x_first else (xp, xm)
        self.c, self.d, self.to_sibling = [None], [], []

    def at(self, near, far, lo, hi):
        x_off, z_off = (near, far) if self.x_first else (far, near)
        x = slice(None) if x_off is None else lax.rem(self.x + x_off + 4, 4)
        zl = slice(None) if z_off is None else lax.rem(self.zl + z_off + 4, 4)
        return self.w.at[self.weight, zl, x, self.core, lo:hi]

    def push(self, part, device):
        return self.net.start(part, part, device)

    def near_send(self, near, far, lo, mid, hi, halves=False):
        if halves:
            return (
                self.push(self.at(-near, far, lo, mid), self.near[0]),
                self.push(self.at(near, far, mid, hi), self.near[1]),
            )
        part = self.at(near, far, lo, hi)
        return (self.push(part, self.near[0]), self.push(part, self.near[1]))

    def far_send(self, near):
        part = self.at(near, 0, self.first, self.end)
        return (self.push(part, self.far[0]), self.push(part, self.far[1]))

    def far_pass(self, near):
        return (
            self.push(self.at(near, -1, self.first, self.mid), self.far[0]),
            self.push(self.at(near, 1, self.mid, self.end), self.far[1]),
        )

    def start_near(self):
        self.a = self.near_send(0, 0, self.first, self.mid, self.end)

    def start_far(self):
        self.c[0] = self.far_send(0)

    def e1(self):
        lo, mid, hi = self.first, self.mid, self.end
        self.wait(self.a)
        self.b = self.near_send(1, 0, lo, mid, hi, halves=True)
        self.c += [self.far_send(-1), self.far_send(1)]
        self.sib(self.at(-1, 0, lo, hi))
        self.sib(self.at(1, 0, lo, hi))

    def e2(self):
        self.wait(self.b)
        self.c.append(self.far_send(2))
        self.sib(self.at(2, 0, self.first, self.end))

    def e3(self):
        self.wait(self.c[0])
        self.d.append(self.far_pass(0))

    def e4(self):
        self.wait(self.c[1])
        self.wait(self.c[2])
        self.d += [self.far_pass(-1), self.far_pass(1)]

    def e5(self):
        self.wait(self.c[3])
        self.d.append(self.far_pass(2))
        self.sib(self.at(None, -1, self.first, self.end))
        self.sib(self.at(None, 1, self.first, self.end))

    def e6(self):
        for pair in self.d:
            self.wait(pair)
        self.sib(self.at(None, 2, self.first, self.end))

    def e7(self):
        self.from_sibling(0, 6)

    def from_sibling(self, first, end):
        for copy in self.to_sibling[first:end]:
            copy.wait_recv()

    def wait(self, pair):
        for copy in pair:
            copy.wait_recv()

    def sib(self, part):
        self.to_sibling.append(self.push(part, self.sibling))


def kernel(
    traded_ref,
    lengths_ref,
    tokens_ref,
    ids_ref,
    freq_ref,
    cache_ref,
    wq_ref,
    wk_ref,
    wv_ref,
    wo_ref,
    gate_ref,
    up_ref,
    down_ref,
    out_ref,
    w,
    qkv_w,
    o_w,
    cache,
    other_tokens,
    other_ids,
    normed,
    query,
    key,
    value,
    cosine,
    sine,
    bias,
    mixed,
    terms,
    send_one,
    recv_one,
    state,
    normed_two,
    hidden,
    sums,
    send_two,
    recv_two,
    done,
    other_done,
    send_sem,
    recv_sem,
    local_sem,
):
    rep, dp, mp = lax.axis_index("rep"), lax.axis_index("dp"), lax.axis_index("mp")
    zl, x, core = dp // 8, lax.rem(dp // 2, 4), lax.rem(dp, 2)
    z = rep * 4 + zl

    def at_z(where):
        where = lax.rem(where + 8, 8)
        return (where // 4, (lax.rem(where, 4) * 4 + x) * 2 + core, mp)

    def at_x(where):
        return (rep, (zl * 4 + lax.rem(where + 4, 4)) * 2 + core, mp)

    sibling = (rep, (zl * 4 + x) * 2 + (1 - core), mp)
    partner = (1 - rep, dp, mp)
    peers = [(rep, dp, lax.rem(mp + k, 4)) for k in (1, 2, 3)]
    around = (at_x(x + 1), at_x(x - 1), at_z(z + 1), at_z(z - 1), sibling)

    locals_ = []

    def fetch(src, dst):
        copy = pltpu.make_async_copy(src, dst, local_sem.at[len(locals_)])
        locals_.append(copy)
        copy.start()
        return copy

    shards = [
        fetch(ref, w.at[i, zl, x, core]) for i, ref in enumerate((gate_ref, up_ref, down_ref))
    ]

    barrier = pltpu.get_barrier_semaphore()
    friends = peers + [partner] + list(around)
    for friend in friends:
        pl.semaphore_signal(barrier, inc=1, device_id=friend, device_id_type=MESH)
    pl.semaphore_wait(barrier, len(friends))

    net = Copies(send_sem, recv_sem)

    def serve(place):
        for step in PLAN[place]:
            name, call = step.split(".")
            if call in SIBLING:
                streams[name].from_sibling(*SIBLING[call])
            else:
                getattr(streams[name], call)()

    swap_ids = net.start(ids_ref, other_ids, partner)
    swaps = []
    for chunk in range(CHUNKS):
        rows = slice(chunk * CHUNK, (chunk + 1) * CHUNK)
        swaps.append(net.start(tokens_ref.at[rows], other_tokens.at[rows], partner))
    cache_rows = pl.ds(pl.multiple_of(mp * 128, 128), 128)
    cache_copies = []
    for k in (2, 1, 3, 0):
        to = lax.rem(mp + k, 4)
        for i in range(2):
            columns = pl.ds(pl.multiple_of(i * D + to * WIDTH, WIDTH), WIDTH)
            src, dst = cache_ref.at[:, columns], cache.at[i, cache_rows]
            if k == 0:
                cache_copies.append(fetch(src, dst))
            else:
                cache_copies.append(net.start(src, dst, peers[k - 1]))
    for copy in shards:
        copy.wait()
    streams = {
        name: Stream(spec, net, w, (zl, x, core), around) for name, spec in zip("gud", STREAMS)
    }
    serve("issue")
    own_shard = w.at[:, zl, x, core]
    sib_own = net.start(own_shard, own_shard, sibling)
    qkv_copies = [fetch(ref, qkv_w.at[i]) for i, ref in enumerate((wq_ref, wk_ref, wv_ref))]
    o_copy = fetch(wo_ref, o_w)
    swap_ids.wait_recv()

    def kept_at(half, m):
        return slice(half * HALF + m * PART, half * HALF + (m + 1) * PART)

    def token_at(half, m):
        return slice(m * OWN + half * PART, m * OWN + (half + 1) * PART)

    blocks = [(half, m) for half in range(2) for m in range(4)]
    moved = traded_ref[0] == 1
    group = rep * 32 + dp
    ids = jnp.where(moved, other_ids[...], ids_ref[...])
    place = lax.broadcasted_iota(jnp.int32, (1, GROUP), 1)
    positions = place
    cached_place = lax.broadcasted_iota(jnp.int32, (1, CACHE), 1)
    owner = jnp.zeros((1, CACHE), jnp.int32)
    bound = 0
    for s in range(REQS):
        length = lengths_ref[s, group]
        start = jnp.sum((ids < s).astype(jnp.int32), axis=1, keepdims=True)
        positions = positions + jnp.where(ids == s, length - start, 0)
        bound = bound + length
        owner = owner + (cached_place >= bound).astype(jnp.int32)
    ids_column = jnp.transpose(jnp.broadcast_to(ids.astype(jnp.float32), (128, GROUP)))
    places_column = jnp.transpose(jnp.broadcast_to(positions.astype(jnp.float32), (128, GROUP)))
    angle = places_column * freq_ref[...]
    cosine[...] = jnp.cos(angle)
    lane = lax.broadcasted_iota(jnp.int32, (GROUP, HEAD_DIM), 1)
    wave = jnp.sin(angle)
    sine[...] = jnp.where(lane < HEAD_DIM // 2, -wave, wave)
    owner = owner.astype(jnp.float32)
    ids_row = ids.astype(jnp.float32)
    for half, m in blocks:
        column = ids_column[token_at(half, m), :1]
        kept = kept_at(half, m)
        bias[kept, :CACHE] = jnp.where(column == owner, 0.0, -1e30)
        row_at = lax.broadcasted_iota(jnp.int32, (PART, GROUP), 0) + token_at(half, m).start
        column_at = lax.broadcasted_iota(jnp.int32, (PART, GROUP), 1)
        same = (column == ids_row) & (column_at <= row_at)
        bias[kept, CACHE:] = jnp.where(same, 0.0, -1e30)

    gathers = []
    for chunk in range(CHUNKS):
        rows = slice(chunk * CHUNK, (chunk + 1) * CHUNK)
        swaps[chunk].wait_recv()
        tokens = jnp.where(moved, other_tokens[rows, :], tokens_ref[rows, :])
        kept = pl.ds(pl.multiple_of(mp * OWN + chunk * CHUNK, CHUNK), CHUNK)
        normed[kept, :] = normalize(tokens.astype(jnp.float32)).astype(jnp.bfloat16)
        for k in (2, 1, 3):
            gathers.append(net.start(normed.at[kept], normed.at[kept], peers[k - 1]))
        serve(f"swap{chunk}")
    for copy in gathers:
        copy.wait_recv()
    for copy in qkv_copies:
        copy.wait()
    serve("ag1")
    @pl.loop(0, HEADS // 2)
    def _(pair):
        columns = pl.ds(pl.multiple_of(pair * 256, 256), 256)
        rows = normed[...]
        q = dot(rows, qkv_w[0, :, columns])
        k = dot(rows, qkv_w[1, :, columns])
        v = dot(rows, qkv_w[2, :, columns])
        value[:, columns] = v.astype(jnp.bfloat16)
        for side in range(2):
            part = slice(side * HEAD_DIM, (side + 1) * HEAD_DIM)
            lanes = pl.ds(pl.multiple_of(pair * 256 + side * HEAD_DIM, HEAD_DIM), HEAD_DIM)
            turned = k[:, part] * cosine[...] + pltpu.roll(k[:, part], HEAD_DIM // 2, 1) * sine[...]
            key[:, lanes] = turned.astype(jnp.bfloat16)
            turned = q[:, part] * cosine[...] + pltpu.roll(q[:, part], HEAD_DIM // 2, 1) * sine[...]
            turned = turned.astype(jnp.bfloat16)
            for half, m in blocks:
                query[kept_at(half, m), lanes] = turned[token_at(half, m)]

    serve("qkv")
    for copy in cache_copies[:-2]:
        copy.wait_recv()
    for copy in cache_copies[-2:]:
        copy.wait()
    o_copy.wait()

    scale = 1.0 / math.sqrt(HEAD_DIM)
    own_part = [
        pl.ds(pl.multiple_of(half * HALF + mp * PART, PART), PART) for half in range(2)
    ]

    def attend(half):
        @pl.loop(0, HEADS)
        def _(h):
            columns = pl.ds(pl.multiple_of(h * HEAD_DIM, HEAD_DIM), HEAD_DIM)
            inner = (((1,), (1,)), ((), ()))
            for block in range(2):
                rows = slice(half * HALF + block * 96, half * HALF + block * 96 + 96)
                q = query[rows, columns]
                old = dot(q, cache[0, :, columns], inner) * scale + bias[rows, :CACHE]
                new = dot(q, key[:, columns], inner) * scale + bias[rows, CACHE:]
                top = jnp.maximum(
                    jnp.max(old, axis=1, keepdims=True), jnp.max(new, axis=1, keepdims=True)
                )
                old, new = jnp.exp(old - top), jnp.exp(new - top)
                total = jnp.sum(old, axis=1, keepdims=True) + jnp.sum(new, axis=1, keepdims=True)
                share = 1.0 / total
                out = dot((old * share).astype(jnp.bfloat16), cache[1, :, columns])
                out = out + dot((new * share).astype(jnp.bfloat16), value[:, columns])
                mixed[rows, columns] = out.astype(jnp.bfloat16)

    def scatter(half, columns, send, recv):
        copies = []
        for k in (2, 1, 3):
            rows = pl.ds(pl.multiple_of(half * HALF + lax.rem(mp + k, 4) * PART, PART), PART)
            copies.append(
                net.start(
                    send.at[rows, columns],
                    recv.at[k - 1, half * PART : (half + 1) * PART, columns],
                    peers[k - 1],
                )
            )
        return copies

    def collect(half, columns, copies, recv):
        for copy in copies:
            copy.wait_recv()
        total = terms[own_part[half], columns]
        for k in range(3):
            total = total + recv[k, half * PART : (half + 1) * PART, columns].astype(jnp.float32)
        return total

    def project(half):
        rows = slice(half * HALF, (half + 1) * HALF)
        for tile in range(4):
            columns = slice(tile * 512, (tile + 1) * 512)
            part = dot(mixed[rows, :], o_w[:, columns])
            terms[rows, columns] = part
            send_one[rows, columns] = part.astype(jnp.bfloat16)
        return scatter(half, slice(0, D), send_one, recv_one)

    scattered = []
    for half in range(2):
        attend(half)
        scattered.append(project(half))
        serve(f"attn{half}")


    gathers = []
    for half in range(2):
        rows = slice(half * PART, (half + 1) * PART)
        own = jnp.where(moved, other_tokens[rows, :], tokens_ref[rows, :])
        total = collect(half, slice(0, D), scattered[half], recv_one)
        fresh = (own.astype(jnp.float32) + total).astype(jnp.bfloat16)
        state[rows, :] = fresh
        kept = own_part[half]
        normed_two[kept, :] = normalize(fresh.astype(jnp.float32)).astype(jnp.bfloat16)
        gathers.append(
            [net.start(normed_two.at[kept], normed_two.at[kept], peers[k - 1]) for k in (2, 1, 3)]
        )
        serve(f"rs{half}")

    sib_own.wait_recv()
    serve("ag2")
    def raise_up(half):
        for copy in gathers[half]:
            copy.wait_recv()

        @pl.loop(0, FF // 512)
        def _(tile):
            columns = pl.ds(pl.multiple_of(tile * 512, 512), 512)
            rows = normed_two[half * HALF : (half + 1) * HALF, :]
            gate = dot(rows, w[0, :, :, :, :, columns].reshape(D, 512))
            upward = dot(rows, w[1, :, :, :, :, columns].reshape(D, 512))
            hidden[half * HALF : (half + 1) * HALF, columns] = (
                gate / (1.0 + jnp.exp(-gate)) * upward
            ).astype(jnp.bfloat16)

    raise_up(0)
    serve("up0")
    raise_up(1)
    serve("up1")
    units = [(tile, half) for tile in range(4) for half in range(2)]
    scattered = []
    returns = []

    def features(tile):
        at = lax.rem(x + (0, -1, 1, 2)[tile] + 4, 4)
        return [pl.ds(pl.multiple_of(zone * 512 + at * 128, 128), 128) for zone in range(4)]

    def give_back(unit):
        tile, half = units[unit]
        rows = slice(half * PART, (half + 1) * PART)
        for copy in scattered[unit]:
            copy.wait_recv()
        total = sums[tile, own_part[half]]
        for k in range(3):
            total = total + recv_two[k, tile, rows].astype(jnp.float32)
        base = jnp.concatenate([state[rows, lanes] for lanes in features(tile)], axis=1)
        done[tile, rows] = (base.astype(jnp.float32) + total).astype(jnp.bfloat16)
        part = net.start(done.at[tile, rows], other_done.at[tile, rows], partner)
        returns.append((tile, rows, part))

    serve("tile0")
    for unit, (tile, half) in enumerate(units):
        if half == 0 and tile in (1, 3):
            serve(f"tile{tile}")
        at = lax.rem(x + (0, -1, 1, 2)[tile] + 4, 4)
        rows = slice(half * HALF, (half + 1) * HALF)
        matrix = w[2, :, at].reshape(TILE, FF)
        part = dot(hidden[rows, :], matrix, (((1,), (1,)), ((), ())))
        sums[tile, rows] = part
        send_two[tile, rows] = part.astype(jnp.bfloat16)
        copies = []
        for k in (2, 1, 3):
            theirs = pl.ds(
                pl.multiple_of(half * HALF + lax.rem(mp + k, 4) * PART, PART), PART
            )
            target = recv_two.at[k - 1, tile, half * PART : (half + 1) * PART]
            copies.append(net.start(send_two.at[tile, theirs], target, peers[k - 1]))
        scattered.append(copies)
        if unit >= LAG:
            give_back(unit - LAG)
    for unit in range(len(units) - LAG, len(units)):
        give_back(unit)
    for tile, rows, part in returns:
        part.wait_recv()
        chosen = jnp.where(moved, other_done[tile, rows], done[tile, rows])
        for zone, lanes in enumerate(features(tile)):
            out_ref[rows, lanes] = chosen[:, zone * 128 : (zone + 1) * 128]
    for copy in net.all:
        if all(copy is not gone for gone in net.gone):
            copy.wait_send()


N_COPIES = 11 + 3 * CHUNKS + N_STREAM_COPIES * 3 + 12 + 32 + CHUNKS


def local(
    tokens,
    request_ids,
    cache_entries,
    cached_lengths,
    traded,
    query_weight,
    key_weight,
    value_weight,
    output_weight,
    gate_weight,
    up_weight,
    down_weight,
):
    half = HEAD_DIM // 2
    freq = ROPE_BASE ** (-np.arange(half, dtype=np.float64) / half)
    freq = jnp.asarray(np.concatenate([freq, freq])[None].astype(np.float32))
    bf16, f32 = jnp.bfloat16, jnp.float32
    in_vmem = pl.BlockSpec(memory_space=pltpu.VMEM)
    in_smem = pl.BlockSpec(memory_space=pltpu.SMEM)
    in_hbm = pl.BlockSpec(memory_space=pl.ANY)
    return pl.pallas_call(
        kernel,
        out_shape=jax.ShapeDtypeStruct((OWN, D), bf16),
        in_specs=[in_smem, in_smem, in_vmem, in_vmem, in_vmem] + [in_hbm] * 8,
        out_specs=in_vmem,
        scratch_shapes=[
            pltpu.VMEM((3, 4, 4, 2, 64, D), bf16),
            pltpu.VMEM((3, D, WIDTH), bf16),
            pltpu.VMEM((WIDTH, D), bf16),
            pltpu.VMEM((2, CACHE, WIDTH), bf16),
            pltpu.VMEM((OWN, D), bf16),
            pltpu.VMEM((1, GROUP), jnp.int32),
            pltpu.VMEM((GROUP, D), bf16),
            pltpu.VMEM((GROUP, WIDTH), bf16),
            pltpu.VMEM((GROUP, WIDTH), bf16),
            pltpu.VMEM((GROUP, WIDTH), bf16),
            pltpu.VMEM((GROUP, HEAD_DIM), f32),
            pltpu.VMEM((GROUP, HEAD_DIM), f32),
            pltpu.VMEM((GROUP, CACHE + GROUP), f32),
            pltpu.VMEM((GROUP, WIDTH), bf16),
            pltpu.VMEM((GROUP, D), f32),
            pltpu.VMEM((GROUP, D), bf16),
            pltpu.VMEM((3, OWN, D), bf16),
            pltpu.VMEM((OWN, D), bf16),
            pltpu.VMEM((GROUP, D), bf16),
            pltpu.VMEM((GROUP, FF), bf16),
            pltpu.VMEM((4, GROUP, TILE), f32),
            pltpu.VMEM((4, GROUP, TILE), bf16),
            pltpu.VMEM((3, 4, OWN, TILE), bf16),
            pltpu.VMEM((4, OWN, TILE), bf16),
            pltpu.VMEM((4, OWN, TILE), bf16),
            pltpu.SemaphoreType.DMA((N_COPIES,)),
            pltpu.SemaphoreType.DMA((N_COPIES,)),
            pltpu.SemaphoreType.DMA((9,)),
        ],
        compiler_params=pltpu.CompilerParams(
            collective_id=0, has_side_effects=True, vmem_limit_bytes=60 * 1024 * 1024
        ),
        name="layer",
    )(
        traded,
        cached_lengths.T,
        tokens,
        request_ids,
        freq,
        cache_entries,
        query_weight,
        key_weight,
        value_weight,
        output_weight,
        gate_weight,
        up_weight,
        down_weight,
    )


def solution(mesh):
    in_specs = (
        P(("rep", "dp", "mp"), None),
        P(("rep", "dp"), None),
        P(("rep", "dp", "mp"), None),
        P(),
        P("dp"),
        P(None, "mp"),
        P(None, "mp"),
        P(None, "mp"),
        P("mp", None),
        P("dp", "mp"),
        P("dp", "mp"),
        P("dp", "mp"),
    )
    out_specs = P(("rep", "dp", "mp"), None)
    return jax.shard_map(local, mesh=mesh, in_specs=in_specs, out_specs=out_specs, check_vma=False)
```

```python
import functools
import math

import jax
import jax.numpy as jnp
import numpy as np
from jax import lax
from jax.experimental import pallas as pl
from jax.experimental.pallas import tpu as pltpu
from jax.sharding import PartitionSpec as P

D = 2048
FF = 2048
HEADS = 4
HEAD_DIM = 128
WIDTH = HEADS * HEAD_DIM
GROUP = 384
OWN = 96
CACHE = 512
REQS = 8
EPSILON = 1e-05
ROPE_BASE = 10000.0
MESH = pl.DeviceIdType.MESH

STREAMS = ((0, 0, 64, True), (1, 0, 64, False), (2, 0, 64, False))
SIBLING = {"s0": (0, 3), "s1": (3, 5), "s2": (5, 6)}
PLAN = {
    "issue": ("g.start_near", "u.start_far", "g.start_far", "d.start_far",),
    "swap0": (),
    "swap1": ("u.start_near",),
    "swap2": ("g.e1",),
    "ag1": ("g.e2", "u.e3",),
    "qkv": ("u.e1", "g.e3",),
    "attn0": (),
    "attn1": ("u.e2", "d.start_near",),
    "rs0": ("u.e4",),
    "rs1": ("g.e4", "u.e5",),
    "ag2": ("g.e5", "d.e1", "g.e6", "u.e6", "d.e3", "d.e2", "g.e7", "u.e7",),
    "up0": (),
    "up1": ("d.e4",),
    "tile0": ("d.s0",),
    "tile1": ("d.e5", "d.s1",),
    "tile3": ("d.e6", "d.s2",),
}
N_STREAM_COPIES = 26
HALF = GROUP // 2
PART = OWN // 2
CHUNKS = 3
CHUNK = OWN // CHUNKS
LAG = 2
TILE = 512


def normalize(rows):
    center = rows - jnp.mean(rows, axis=-1, keepdims=True)
    spread = jnp.mean(center * center, axis=-1, keepdims=True)
    return center * lax.rsqrt(spread + EPSILON)


def dot(a, b, dims=(((1,), (0,)), ((), ()))):
    return lax.dot_general(a, b, dims, preferred_element_type=jnp.float32)


class Copies:
    def __init__(self, send, recv):
        self.send, self.recv, self.used, self.all, self.gone = send, recv, 0, [], []

    def start(self, src, dst, device):
        copy = pltpu.make_async_remote_copy(
            src_ref=src,
            dst_ref=dst,
            send_sem=self.send.at[self.used],
            recv_sem=self.recv.at[self.used],
            device_id=device,
            device_id_type=MESH,
        )
        self.used += 1
        self.all.append(copy)
        copy.start()
        return copy

    def leave(self, copies):
        for copy in copies:
            copy.wait_send()
            self.gone.append(copy)


class Stream:
    def __init__(self, spec, net, w_ref, place, neighbours):
        self.weight, self.first, self.end, self.x_first = spec
        self.mid = (self.first + self.end) // 2
        self.net, self.w = net, w_ref
        self.zl, self.x, self.core = place
        xp, xm, zp, zm, self.sibling = neighbours
        self.near = (xp, xm) if self.x_first else (zp, zm)
        self.far = (zp, zm) if self.x_first else (xp, xm)
        self.c, self.d, self.to_sibling = [None], [], []

    def at(self, near, far, lo, hi):
        x_off, z_off = (near, far) if self.x_first else (far, near)
        x = slice(None) if x_off is None else lax.rem(self.x + x_off + 4, 4)
        zl = slice(None) if z_off is None else lax.rem(self.zl + z_off + 4, 4)
        return self.w.at[self.weight, zl, x, self.core, lo:hi]

    def push(self, part, device):
        return self.net.start(part, part, device)

    def near_send(self, near, far, lo, mid, hi, halves=False):
        if halves:
            return (
                self.push(self.at(-near, far, lo, mid), self.near[0]),
                self.push(self.at(near, far, mid, hi), self.near[1]),
            )
        part = self.at(near, far, lo, hi)
        return (self.push(part, self.near[0]), self.push(part, self.near[1]))

    def far_send(self, near):
        part = self.at(near, 0, self.first, self.end)
        return (self.push(part, self.far[0]), self.push(part, self.far[1]))

    def far_pass(self, near):
        return (
            self.push(self.at(near, -1, self.first, self.mid), self.far[0]),
            self.push(self.at(near, 1, self.mid, self.end), self.far[1]),
        )

    def start_near(self):
        self.a = self.near_send(0, 0, self.first, self.mid, self.end)

    def start_far(self):
        self.c[0] = self.far_send(0)

    def e1(self):
        lo, mid, hi = self.first, self.mid, self.end
        self.wait(self.a)
        self.b = self.near_send(1, 0, lo, mid, hi, halves=True)
        self.c += [self.far_send(-1), self.far_send(1)]
        self.sib(self.at(-1, 0, lo, hi))
        self.sib(self.at(1, 0, lo, hi))

    def e2(self):
        self.wait(self.b)
        self.c.append(self.far_send(2))
        self.sib(self.at(2, 0, self.first, self.end))

    def e3(self):
        self.wait(self.c[0])
        self.d.append(self.far_pass(0))

    def e4(self):
        self.wait(self.c[1])
        self.wait(self.c[2])
        self.d += [self.far_pass(-1), self.far_pass(1)]

    def e5(self):
        self.wait(self.c[3])
        self.d.append(self.far_pass(2))
        self.sib(self.at(None, -1, self.first, self.end))
        self.sib(self.at(None, 1, self.first, self.end))

    def e6(self):
        for pair in self.d:
            self.wait(pair)
        self.sib(self.at(None, 2, self.first, self.end))

    def e7(self):
        self.from_sibling(0, 6)

    def from_sibling(self, first, end):
        for copy in self.to_sibling[first:end]:
            copy.wait_recv()

    def wait(self, pair):
        for copy in pair:
            copy.wait_recv()

    def sib(self, part):
        self.to_sibling.append(self.push(part, self.sibling))


def kernel(
    traded_ref,
    lengths_ref,
    tokens_ref,
    ids_ref,
    freq_ref,
    cache_ref,
    wq_ref,
    wk_ref,
    wv_ref,
    wo_ref,
    gate_ref,
    up_ref,
    down_ref,
    out_ref,
    w,
    qkv_w,
    o_w,
    cache,
    other_tokens,
    other_ids,
    normed,
    query,
    key,
    value,
    cosine,
    sine,
    bias,
    mixed,
    terms,
    send_one,
    recv_one,
    state,
    normed_two,
    hidden,
    sums,
    send_two,
    recv_two,
    done,
    other_done,
    send_sem,
    recv_sem,
    local_sem,
):
    rep, dp, mp = lax.axis_index("rep"), lax.axis_index("dp"), lax.axis_index("mp")
    zl, x, core = dp // 8, lax.rem(dp // 2, 4), lax.rem(dp, 2)
    z = rep * 4 + zl

    def at_z(where):
        where = lax.rem(where + 8, 8)
        return (where // 4, (lax.rem(where, 4) * 4 + x) * 2 + core, mp)

    def at_x(where):
        return (rep, (zl * 4 + lax.rem(where + 4, 4)) * 2 + core, mp)

    sibling = (rep, (zl * 4 + x) * 2 + (1 - core), mp)
    partner = (1 - rep, dp, mp)
    peers = [(rep, dp, lax.rem(mp + k, 4)) for k in (1, 2, 3)]
    around = (at_x(x + 1), at_x(x - 1), at_z(z + 1), at_z(z - 1), sibling)

    locals_ = []

    def fetch(src, dst):
        copy = pltpu.make_async_copy(src, dst, local_sem.at[len(locals_)])
        locals_.append(copy)
        copy.start()
        return copy

    shards = [
        fetch(ref, w.at[i, zl, x, core]) for i, ref in enumerate((gate_ref, up_ref, down_ref))
    ]

    barrier = pltpu.get_barrier_semaphore()
    friends = peers + [partner] + list(around)
    for friend in friends:
        pl.semaphore_signal(barrier, inc=1, device_id=friend, device_id_type=MESH)
    pl.semaphore_wait(barrier, len(friends))

    net = Copies(send_sem, recv_sem)

    def serve(place):
        for step in PLAN[place]:
            name, call = step.split(".")
            if call in SIBLING:
                streams[name].from_sibling(*SIBLING[call])
            else:
                getattr(streams[name], call)()

    swap_ids = net.start(ids_ref, other_ids, partner)
    swaps = []
    for chunk in range(CHUNKS):
        rows = slice(chunk * CHUNK, (chunk + 1) * CHUNK)
        swaps.append(net.start(tokens_ref.at[rows], other_tokens.at[rows], partner))
    cache_rows = pl.ds(pl.multiple_of(mp * 128, 128), 128)
    cache_copies = []
    for k in (2, 1, 3, 0):
        to = lax.rem(mp + k, 4)
        for i in range(2):
            columns = pl.ds(pl.multiple_of(i * D + to * WIDTH, WIDTH), WIDTH)
            src, dst = cache_ref.at[:, columns], cache.at[i, cache_rows]
            if k == 0:
                cache_copies.append(fetch(src, dst))
            else:
                cache_copies.append(net.start(src, dst, peers[k - 1]))
    for copy in shards:
        copy.wait()
    streams = {
        name: Stream(spec, net, w, (zl, x, core), around) for name, spec in zip("gud", STREAMS)
    }
    serve("issue")
    own_shard = w.at[:, zl, x, core]
    sib_own = net.start(own_shard, own_shard, sibling)
    qkv_copies = [fetch(ref, qkv_w.at[i]) for i, ref in enumerate((wq_ref, wk_ref, wv_ref))]
    o_copy = fetch(wo_ref, o_w)
    swap_ids.wait_recv()

    def kept_at(half, m):
        return slice(half * HALF + m * PART, half * HALF + (m + 1) * PART)

    def token_at(half, m):
        return slice(m * OWN + half * PART, m * OWN + (half + 1) * PART)

    blocks = [(half, m) for half in range(2) for m in range(4)]
    moved = traded_ref[0] == 1
    group = rep * 32 + dp
    ids = jnp.where(moved, other_ids[...], ids_ref[...])
    place = lax.broadcasted_iota(jnp.int32, (1, GROUP), 1)
    positions = place
    cached_place = lax.broadcasted_iota(jnp.int32, (1, CACHE), 1)
    owner = jnp.zeros((1, CACHE), jnp.int32)
    bound = 0
    for s in range(REQS):
        length = lengths_ref[s, group]
        start = jnp.sum((ids < s).astype(jnp.int32), axis=1, keepdims=True)
        positions = positions + jnp.where(ids == s, length - start, 0)
        bound = bound + length
        owner = owner + (cached_place >= bound).astype(jnp.int32)
    ids_column = jnp.transpose(jnp.broadcast_to(ids.astype(jnp.float32), (128, GROUP)))
    places_column = jnp.transpose(jnp.broadcast_to(positions.astype(jnp.float32), (128, GROUP)))
    angle = places_column * freq_ref[...]
    cosine[...] = jnp.cos(angle)
    lane = lax.broadcasted_iota(jnp.int32, (GROUP, HEAD_DIM), 1)
    wave = jnp.sin(angle)
    sine[...] = jnp.where(lane < HEAD_DIM // 2, -wave, wave)
    owner = owner.astype(jnp.float32)
    ids_row = ids.astype(jnp.float32)
    for half, m in blocks:
        column = ids_column[token_at(half, m), :1]
        kept = kept_at(half, m)
        bias[kept, :CACHE] = jnp.where(column == owner, 0.0, -1e30)
        row_at = lax.broadcasted_iota(jnp.int32, (PART, GROUP), 0) + token_at(half, m).start
        column_at = lax.broadcasted_iota(jnp.int32, (PART, GROUP), 1)
        same = (column == ids_row) & (column_at <= row_at)
        bias[kept, CACHE:] = jnp.where(same, 0.0, -1e30)

    def hand_on(ref, rows, side):
        return net.start(ref.at[rows], ref.at[rows], peers[(0, 2)[side]])

    def neighbour(off, first, count):
        return pl.ds(pl.multiple_of(lax.rem(mp + off + 4, 4) * OWN + first, 16), count)

    gathers = []
    for chunk in range(CHUNKS):
        rows = slice(chunk * CHUNK, (chunk + 1) * CHUNK)
        swaps[chunk].wait_recv()
        tokens = jnp.where(moved, other_tokens[rows, :], tokens_ref[rows, :])
        kept = pl.ds(pl.multiple_of(mp * OWN + chunk * CHUNK, CHUNK), CHUNK)
        normed[kept, :] = normalize(tokens.astype(jnp.float32)).astype(jnp.bfloat16)
        gathers.append([net.start(normed.at[kept], normed.at[kept], peers[k - 1]) for k in (1, 3)])
        if chunk == CHUNKS - 1:
            gathers[0][0].wait_recv()
            passed = [hand_on(normed, neighbour(-1, 0, CHUNK), 0)]
        serve(f"swap{chunk}")
    gathers[1][1].wait_recv()
    passed.append(hand_on(normed, neighbour(1, CHUNK, CHUNK), 1))
    gathers[2][0].wait_recv()
    passed.append(hand_on(normed, neighbour(-1, 2 * CHUNK, CHUNK // 2), 0))
    gathers[2][1].wait_recv()
    passed.append(hand_on(normed, neighbour(1, 2 * CHUNK + CHUNK // 2, CHUNK // 2), 1))
    gathers[0][1].wait_recv()
    gathers[1][0].wait_recv()
    for copy in passed:
        copy.wait_recv()
    for copy in qkv_copies:
        copy.wait()
    serve("ag1")
    @pl.loop(0, HEADS // 2)
    def _(pair):
        columns = pl.ds(pl.multiple_of(pair * 256, 256), 256)
        rows = normed[...]
        q = dot(rows, qkv_w[0, :, columns])
        k = dot(rows, qkv_w[1, :, columns])
        v = dot(rows, qkv_w[2, :, columns])
        value[:, columns] = v.astype(jnp.bfloat16)
        for side in range(2):
            part = slice(side * HEAD_DIM, (side + 1) * HEAD_DIM)
            lanes = pl.ds(pl.multiple_of(pair * 256 + side * HEAD_DIM, HEAD_DIM), HEAD_DIM)
            turned = k[:, part] * cosine[...] + pltpu.roll(k[:, part], HEAD_DIM // 2, 1) * sine[...]
            key[:, lanes] = turned.astype(jnp.bfloat16)
            turned = q[:, part] * cosine[...] + pltpu.roll(q[:, part], HEAD_DIM // 2, 1) * sine[...]
            turned = turned.astype(jnp.bfloat16)
            for half, m in blocks:
                query[kept_at(half, m), lanes] = turned[token_at(half, m)]

    serve("qkv")
    for copy in cache_copies[:-2]:
        copy.wait_recv()
    for copy in cache_copies[-2:]:
        copy.wait()
    o_copy.wait()

    scale = 1.0 / math.sqrt(HEAD_DIM)
    own_part = [
        pl.ds(pl.multiple_of(half * HALF + mp * PART, PART), PART) for half in range(2)
    ]

    def attend(half):
        @pl.loop(0, HEADS)
        def _(h):
            columns = pl.ds(pl.multiple_of(h * HEAD_DIM, HEAD_DIM), HEAD_DIM)
            inner = (((1,), (1,)), ((), ()))
            for block in range(2):
                rows = slice(half * HALF + block * 96, half * HALF + block * 96 + 96)
                q = query[rows, columns]
                old = dot(q, cache[0, :, columns], inner) * scale + bias[rows, :CACHE]
                new = dot(q, key[:, columns], inner) * scale + bias[rows, CACHE:]
                top = jnp.maximum(
                    jnp.max(old, axis=1, keepdims=True), jnp.max(new, axis=1, keepdims=True)
                )
                old, new = jnp.exp(old - top), jnp.exp(new - top)
                total = jnp.sum(old, axis=1, keepdims=True) + jnp.sum(new, axis=1, keepdims=True)
                share = 1.0 / total
                out = dot((old * share).astype(jnp.bfloat16), cache[1, :, columns])
                out = out + dot((new * share).astype(jnp.bfloat16), value[:, columns])
                mixed[rows, columns] = out.astype(jnp.bfloat16)

    def scatter(half, columns, send, recv):
        copies = []
        for k in (2, 1, 3):
            rows = pl.ds(pl.multiple_of(half * HALF + lax.rem(mp + k, 4) * PART, PART), PART)
            copies.append(
                net.start(
                    send.at[rows, columns],
                    recv.at[k - 1, half * PART : (half + 1) * PART, columns],
                    peers[k - 1],
                )
            )
        return copies

    def collect(half, columns, copies, recv):
        for copy in copies:
            copy.wait_recv()
        total = terms[own_part[half], columns]
        for k in range(3):
            total = total + recv[k, half * PART : (half + 1) * PART, columns].astype(jnp.float32)
        return total

    def project(half):
        rows = slice(half * HALF, (half + 1) * HALF)
        for tile in range(4):
            columns = slice(tile * 512, (tile + 1) * 512)
            part = dot(mixed[rows, :], o_w[:, columns])
            terms[rows, columns] = part
            send_one[rows, columns] = part.astype(jnp.bfloat16)
        return scatter(half, slice(0, D), send_one, recv_one)

    scattered = []
    for half in range(2):
        attend(half)
        scattered.append(project(half))
        serve(f"attn{half}")


    gathers = []
    for half in range(2):
        rows = slice(half * PART, (half + 1) * PART)
        own = jnp.where(moved, other_tokens[rows, :], tokens_ref[rows, :])
        total = collect(half, slice(0, D), scattered[half], recv_one)
        fresh = (own.astype(jnp.float32) + total).astype(jnp.bfloat16)
        state[rows, :] = fresh
        kept = own_part[half]
        normed_two[kept, :] = normalize(fresh.astype(jnp.float32)).astype(jnp.bfloat16)
        gathers.append(
            [net.start(normed_two.at[kept], normed_two.at[kept], peers[k - 1]) for k in (1, 3)]
        )
        if half == 0:
            serve("rs0")

    for half, off in enumerate((-1, 1)):
        gathers[half].pop(half).wait_recv()
        theirs = pl.ds(
            pl.multiple_of(half * HALF + lax.rem(mp + off + 4, 4) * PART, PART), PART
        )
        gathers[half].append(hand_on(normed_two, theirs, half))
    serve("rs1")
    sib_own.wait_recv()
    serve("ag2")
    def raise_up(half):
        for copy in gathers[half]:
            copy.wait_recv()

        @pl.loop(0, FF // 512)
        def _(tile):
            columns = pl.ds(pl.multiple_of(tile * 512, 512), 512)
            rows = normed_two[half * HALF : (half + 1) * HALF, :]
            gate = dot(rows, w[0, :, :, :, :, columns].reshape(D, 512))
            upward = dot(rows, w[1, :, :, :, :, columns].reshape(D, 512))
            hidden[half * HALF : (half + 1) * HALF, columns] = (
                gate / (1.0 + jnp.exp(-gate)) * upward
            ).astype(jnp.bfloat16)

    raise_up(0)
    serve("up0")
    raise_up(1)
    serve("up1")
    units = [(tile, half) for tile in range(4) for half in range(2)]
    scattered = []
    returns = []

    def features(tile):
        at = lax.rem(x + (0, -1, 1, 2)[tile] + 4, 4)
        return [pl.ds(pl.multiple_of(zone * 512 + at * 128, 128), 128) for zone in range(4)]

    def give_back(unit):
        tile, half = units[unit]
        rows = slice(half * PART, (half + 1) * PART)
        for copy in scattered[unit]:
            copy.wait_recv()
        total = sums[tile, own_part[half]]
        for k in range(3):
            total = total + recv_two[k, tile, rows].astype(jnp.float32)
        base = jnp.concatenate([state[rows, lanes] for lanes in features(tile)], axis=1)
        done[tile, rows] = (base.astype(jnp.float32) + total).astype(jnp.bfloat16)
        part = net.start(done.at[tile, rows], other_done.at[tile, rows], partner)
        returns.append((tile, rows, part))

    serve("tile0")
    for unit, (tile, half) in enumerate(units):
        if half == 0 and tile in (1, 3):
            serve(f"tile{tile}")
        at = lax.rem(x + (0, -1, 1, 2)[tile] + 4, 4)
        rows = slice(half * HALF, (half + 1) * HALF)
        matrix = w[2, :, at].reshape(TILE, FF)
        part = dot(hidden[rows, :], matrix, (((1,), (1,)), ((), ())))
        sums[tile, rows] = part
        send_two[tile, rows] = part.astype(jnp.bfloat16)
        copies = []
        for k in (2, 1, 3):
            theirs = pl.ds(
                pl.multiple_of(half * HALF + lax.rem(mp + k, 4) * PART, PART), PART
            )
            target = recv_two.at[k - 1, tile, half * PART : (half + 1) * PART]
            copies.append(net.start(send_two.at[tile, theirs], target, peers[k - 1]))
        scattered.append(copies)
        if unit >= LAG:
            give_back(unit - LAG)
    for unit in range(len(units) - LAG, len(units)):
        give_back(unit)
    for tile, rows, part in returns:
        part.wait_recv()
        chosen = jnp.where(moved, other_done[tile, rows], done[tile, rows])
        for zone, lanes in enumerate(features(tile)):
            out_ref[rows, lanes] = chosen[:, zone * 128 : (zone + 1) * 128]
    for copy in net.all:
        if all(copy is not gone for gone in net.gone):
            copy.wait_send()


N_COPIES = 12 + 3 * CHUNKS + N_STREAM_COPIES * 3 + 12 + 32 + CHUNKS


def local(
    tokens,
    request_ids,
    cache_entries,
    cached_lengths,
    traded,
    query_weight,
    key_weight,
    value_weight,
    output_weight,
    gate_weight,
    up_weight,
    down_weight,
):
    half = HEAD_DIM // 2
    freq = ROPE_BASE ** (-np.arange(half, dtype=np.float64) / half)
    freq = jnp.asarray(np.concatenate([freq, freq])[None].astype(np.float32))
    bf16, f32 = jnp.bfloat16, jnp.float32
    in_vmem = pl.BlockSpec(memory_space=pltpu.VMEM)
    in_smem = pl.BlockSpec(memory_space=pltpu.SMEM)
    in_hbm = pl.BlockSpec(memory_space=pl.ANY)
    return pl.pallas_call(
        kernel,
        out_shape=jax.ShapeDtypeStruct((OWN, D), bf16),
        in_specs=[in_smem, in_smem, in_vmem, in_vmem, in_vmem] + [in_hbm] * 8,
        out_specs=in_vmem,
        scratch_shapes=[
            pltpu.VMEM((3, 4, 4, 2, 64, D), bf16),
            pltpu.VMEM((3, D, WIDTH), bf16),
            pltpu.VMEM((WIDTH, D), bf16),
            pltpu.VMEM((2, CACHE, WIDTH), bf16),
            pltpu.VMEM((OWN, D), bf16),
            pltpu.VMEM((1, GROUP), jnp.int32),
            pltpu.VMEM((GROUP, D), bf16),
            pltpu.VMEM((GROUP, WIDTH), bf16),
            pltpu.VMEM((GROUP, WIDTH), bf16),
            pltpu.VMEM((GROUP, WIDTH), bf16),
            pltpu.VMEM((GROUP, HEAD_DIM), f32),
            pltpu.VMEM((GROUP, HEAD_DIM), f32),
            pltpu.VMEM((GROUP, CACHE + GROUP), f32),
            pltpu.VMEM((GROUP, WIDTH), bf16),
            pltpu.VMEM((GROUP, D), f32),
            pltpu.VMEM((GROUP, D), bf16),
            pltpu.VMEM((3, OWN, D), bf16),
            pltpu.VMEM((OWN, D), bf16),
            pltpu.VMEM((GROUP, D), bf16),
            pltpu.VMEM((GROUP, FF), bf16),
            pltpu.VMEM((4, GROUP, TILE), f32),
            pltpu.VMEM((4, GROUP, TILE), bf16),
            pltpu.VMEM((3, 4, OWN, TILE), bf16),
            pltpu.VMEM((4, OWN, TILE), bf16),
            pltpu.VMEM((4, OWN, TILE), bf16),
            pltpu.SemaphoreType.DMA((N_COPIES,)),
            pltpu.SemaphoreType.DMA((N_COPIES,)),
            pltpu.SemaphoreType.DMA((9,)),
        ],
        compiler_params=pltpu.CompilerParams(
            collective_id=0, has_side_effects=True, vmem_limit_bytes=60 * 1024 * 1024
        ),
        name="layer",
    )(
        traded,
        cached_lengths.T,
        tokens,
        request_ids,
        freq,
        cache_entries,
        query_weight,
        key_weight,
        value_weight,
        output_weight,
        gate_weight,
        up_weight,
        down_weight,
    )


def solution(mesh):
    in_specs = (
        P(("rep", "dp", "mp"), None),
        P(("rep", "dp"), None),
        P(("rep", "dp", "mp"), None),
        P(),
        P("dp"),
        P(None, "mp"),
        P(None, "mp"),
        P(None, "mp"),
        P("mp", None),
        P("dp", "mp"),
        P("dp", "mp"),
        P("dp", "mp"),
    )
    out_specs = P(("rep", "dp", "mp"), None)
    return jax.shard_map(local, mesh=mesh, in_specs=in_specs, out_specs=out_specs, check_vma=False)
```

```python
import functools
import math

import jax
import jax.numpy as jnp
import numpy as np
from jax import lax
from jax.experimental import pallas as pl
from jax.experimental.pallas import tpu as pltpu
from jax.sharding import PartitionSpec as P

D = 2048
FF = 2048
HEADS = 4
HEAD_DIM = 128
WIDTH = HEADS * HEAD_DIM
GROUP = 384
OWN = 96
CACHE = 512
REQS = 8
EPSILON = 1e-05
ROPE_BASE = 10000.0
MESH = pl.DeviceIdType.MESH

STREAMS = ((0, 0, 64, True), (1, 0, 64, False), (2, 0, 64, False))
SIBLING = {"s0": (0, 3), "s1": (3, 5), "s2": (5, 6)}
PLAN = {
    "issue": ("g.start_near", "u.start_far", "g.start_far", "d.start_far",),
    "swap0": (),
    "swap1": ("u.start_near",),
    "swap2": ("g.e1",),
    "ag1": ("g.e2", "u.e3",),
    "qkv": ("u.e1", "g.e3",),
    "attn0": (),
    "attn1": ("u.e2", "d.start_near",),
    "rs0": ("u.e4",),
    "rs1": ("g.e4", "u.e5",),
    "ag2": ("g.e5", "d.e1", "g.e6", "u.e6", "d.e3", "d.e2", "g.e7", "u.e7",),
    "up0": (),
    "up1": ("d.e4",),
    "tile0": ("d.s0",),
    "tile1": ("d.e5", "d.s1",),
    "tile3": ("d.e6", "d.s2",),
}
N_STREAM_COPIES = 26
HALF = GROUP // 2
PART = OWN // 2
CHUNKS = 3
CHUNK = OWN // CHUNKS
LAG = 3
TILE = 512


def normalize(rows):
    center = rows - jnp.mean(rows, axis=-1, keepdims=True)
    spread = jnp.mean(center * center, axis=-1, keepdims=True)
    return center * lax.rsqrt(spread + EPSILON)


def dot(a, b, dims=(((1,), (0,)), ((), ()))):
    return lax.dot_general(a, b, dims, preferred_element_type=jnp.float32)


class Copies:
    def __init__(self, send, recv):
        self.send, self.recv, self.used, self.all, self.gone = send, recv, 0, [], []

    def start(self, src, dst, device):
        copy = pltpu.make_async_remote_copy(
            src_ref=src,
            dst_ref=dst,
            send_sem=self.send.at[self.used],
            recv_sem=self.recv.at[self.used],
            device_id=device,
            device_id_type=MESH,
        )
        self.used += 1
        self.all.append(copy)
        copy.start()
        return copy

    def leave(self, copies):
        for copy in copies:
            copy.wait_send()
            self.gone.append(copy)


class Stream:
    def __init__(self, spec, net, w_ref, place, neighbours):
        self.weight, self.first, self.end, self.x_first = spec
        self.mid = (self.first + self.end) // 2
        self.net, self.w = net, w_ref
        self.zl, self.x, self.core = place
        xp, xm, zp, zm, self.sibling = neighbours
        self.near = (xp, xm) if self.x_first else (zp, zm)
        self.far = (zp, zm) if self.x_first else (xp, xm)
        self.c, self.d, self.to_sibling = [None], [], []

    def at(self, near, far, lo, hi):
        x_off, z_off = (near, far) if self.x_first else (far, near)
        x = slice(None) if x_off is None else lax.rem(self.x + x_off + 4, 4)
        zl = slice(None) if z_off is None else lax.rem(self.zl + z_off + 4, 4)
        return self.w.at[self.weight, zl, x, self.core, lo:hi]

    def push(self, part, device):
        return self.net.start(part, part, device)

    def near_send(self, near, far, lo, mid, hi, halves=False):
        if halves:
            return (
                self.push(self.at(-near, far, lo, mid), self.near[0]),
                self.push(self.at(near, far, mid, hi), self.near[1]),
            )
        part = self.at(near, far, lo, hi)
        return (self.push(part, self.near[0]), self.push(part, self.near[1]))

    def far_send(self, near):
        part = self.at(near, 0, self.first, self.end)
        return (self.push(part, self.far[0]), self.push(part, self.far[1]))

    def far_pass(self, near):
        return (
            self.push(self.at(near, -1, self.first, self.mid), self.far[0]),
            self.push(self.at(near, 1, self.mid, self.end), self.far[1]),
        )

    def start_near(self):
        self.a = self.near_send(0, 0, self.first, self.mid, self.end)

    def start_far(self):
        self.c[0] = self.far_send(0)

    def e1(self):
        lo, mid, hi = self.first, self.mid, self.end
        self.wait(self.a)
        self.b = self.near_send(1, 0, lo, mid, hi, halves=True)
        self.c += [self.far_send(-1), self.far_send(1)]
        self.sib(self.at(-1, 0, lo, hi))
        self.sib(self.at(1, 0, lo, hi))

    def e2(self):
        self.wait(self.b)
        self.c.append(self.far_send(2))
        self.sib(self.at(2, 0, self.first, self.end))

    def e3(self):
        self.wait(self.c[0])
        self.d.append(self.far_pass(0))

    def e4(self):
        self.wait(self.c[1])
        self.wait(self.c[2])
        self.d += [self.far_pass(-1), self.far_pass(1)]

    def e5(self):
        self.wait(self.c[3])
        self.d.append(self.far_pass(2))
        self.sib(self.at(None, -1, self.first, self.end))
        self.sib(self.at(None, 1, self.first, self.end))

    def e6(self):
        for pair in self.d:
            self.wait(pair)
        self.sib(self.at(None, 2, self.first, self.end))

    def e7(self):
        self.from_sibling(0, 6)

    def from_sibling(self, first, end):
        for copy in self.to_sibling[first:end]:
            copy.wait_recv()

    def wait(self, pair):
        for copy in pair:
            copy.wait_recv()

    def sib(self, part):
        self.to_sibling.append(self.push(part, self.sibling))


def kernel(
    traded_ref,
    lengths_ref,
    tokens_ref,
    ids_ref,
    freq_ref,
    cache_ref,
    wq_ref,
    wk_ref,
    wv_ref,
    wo_ref,
    gate_ref,
    up_ref,
    down_ref,
    out_ref,
    w,
    qkv_w,
    o_w,
    cache,
    other_tokens,
    other_ids,
    normed,
    query,
    key,
    value,
    cosine,
    sine,
    bias,
    mixed,
    terms,
    send_one,
    recv_one,
    state,
    normed_two,
    hidden,
    sums,
    send_two,
    recv_two,
    done,
    other_done,
    send_sem,
    recv_sem,
    local_sem,
):
    rep, dp, mp = lax.axis_index("rep"), lax.axis_index("dp"), lax.axis_index("mp")
    zl, x, core = dp // 8, lax.rem(dp // 2, 4), lax.rem(dp, 2)
    z = rep * 4 + zl

    def at_z(where):
        where = lax.rem(where + 8, 8)
        return (where // 4, (lax.rem(where, 4) * 4 + x) * 2 + core, mp)

    def at_x(where):
        return (rep, (zl * 4 + lax.rem(where + 4, 4)) * 2 + core, mp)

    sibling = (rep, (zl * 4 + x) * 2 + (1 - core), mp)
    partner = (1 - rep, dp, mp)
    peers = [(rep, dp, lax.rem(mp + k, 4)) for k in (1, 2, 3)]
    around = (at_x(x + 1), at_x(x - 1), at_z(z + 1), at_z(z - 1), sibling)

    locals_ = []

    def fetch(src, dst):
        copy = pltpu.make_async_copy(src, dst, local_sem.at[len(locals_)])
        locals_.append(copy)
        copy.start()
        return copy

    shards = [
        fetch(ref, w.at[i, zl, x, core]) for i, ref in enumerate((gate_ref, up_ref, down_ref))
    ]

    barrier = pltpu.get_barrier_semaphore()
    friends = peers + [partner] + list(around)
    for friend in friends:
        pl.semaphore_signal(barrier, inc=1, device_id=friend, device_id_type=MESH)
    pl.semaphore_wait(barrier, len(friends))

    net = Copies(send_sem, recv_sem)

    def serve(place):
        for step in PLAN[place]:
            name, call = step.split(".")
            if call in SIBLING:
                streams[name].from_sibling(*SIBLING[call])
            else:
                getattr(streams[name], call)()

    swap_ids = net.start(ids_ref, other_ids, partner)
    swaps = []
    for chunk in range(CHUNKS):
        rows = slice(chunk * CHUNK, (chunk + 1) * CHUNK)
        swaps.append(net.start(tokens_ref.at[rows], other_tokens.at[rows], partner))
    cache_rows = pl.ds(pl.multiple_of(mp * 128, 128), 128)
    cache_copies = []
    for k in (2, 1, 3, 0):
        to = lax.rem(mp + k, 4)
        for i in range(2):
            columns = pl.ds(pl.multiple_of(i * D + to * WIDTH, WIDTH), WIDTH)
            src, dst = cache_ref.at[:, columns], cache.at[i, cache_rows]
            if k == 0:
                cache_copies.append(fetch(src, dst))
            else:
                cache_copies.append(net.start(src, dst, peers[k - 1]))
    for copy in shards:
        copy.wait()
    streams = {
        name: Stream(spec, net, w, (zl, x, core), around) for name, spec in zip("gud", STREAMS)
    }
    serve("issue")
    own_shard = w.at[:, zl, x, core]
    sib_own = net.start(own_shard, own_shard, sibling)
    qkv_copies = [fetch(ref, qkv_w.at[i]) for i, ref in enumerate((wq_ref, wk_ref, wv_ref))]
    o_copy = fetch(wo_ref, o_w)
    swap_ids.wait_recv()

    def kept_at(half, m):
        return slice(half * HALF + m * PART, half * HALF + (m + 1) * PART)

    def token_at(half, m):
        return slice(m * OWN + half * PART, m * OWN + (half + 1) * PART)

    blocks = [(half, m) for half in range(2) for m in range(4)]
    moved = traded_ref[0] == 1
    group = rep * 32 + dp
    ids = jnp.where(moved, other_ids[...], ids_ref[...])
    place = lax.broadcasted_iota(jnp.int32, (1, GROUP), 1)
    positions = place
    cached_place = lax.broadcasted_iota(jnp.int32, (1, CACHE), 1)
    owner = jnp.zeros((1, CACHE), jnp.int32)
    bound = 0
    for s in range(REQS):
        length = lengths_ref[s, group]
        start = jnp.sum((ids < s).astype(jnp.int32), axis=1, keepdims=True)
        positions = positions + jnp.where(ids == s, length - start, 0)
        bound = bound + length
        owner = owner + (cached_place >= bound).astype(jnp.int32)
    ids_column = jnp.transpose(jnp.broadcast_to(ids.astype(jnp.float32), (128, GROUP)))
    places_column = jnp.transpose(jnp.broadcast_to(positions.astype(jnp.float32), (128, GROUP)))
    angle = places_column * freq_ref[...]
    cosine[...] = jnp.cos(angle)
    lane = lax.broadcasted_iota(jnp.int32, (GROUP, HEAD_DIM), 1)
    wave = jnp.sin(angle)
    sine[...] = jnp.where(lane < HEAD_DIM // 2, -wave, wave)
    owner = owner.astype(jnp.float32)
    ids_row = ids.astype(jnp.float32)
    for half, m in blocks:
        column = ids_column[token_at(half, m), :1]
        kept = kept_at(half, m)
        bias[kept, :CACHE] = jnp.where(column == owner, 0.0, -1e30)
        row_at = lax.broadcasted_iota(jnp.int32, (PART, GROUP), 0) + token_at(half, m).start
        column_at = lax.broadcasted_iota(jnp.int32, (PART, GROUP), 1)
        same = (column == ids_row) & (column_at <= row_at)
        bias[kept, CACHE:] = jnp.where(same, 0.0, -1e30)

    def hand_on(ref, rows, side):
        return net.start(ref.at[rows], ref.at[rows], peers[(0, 2)[side]])

    def neighbour(off, first, count):
        return pl.ds(pl.multiple_of(lax.rem(mp + off + 4, 4) * OWN + first, 16), count)

    gathers = []
    for chunk in range(CHUNKS):
        rows = slice(chunk * CHUNK, (chunk + 1) * CHUNK)
        swaps[chunk].wait_recv()
        tokens = jnp.where(moved, other_tokens[rows, :], tokens_ref[rows, :])
        kept = pl.ds(pl.multiple_of(mp * OWN + chunk * CHUNK, CHUNK), CHUNK)
        normed[kept, :] = normalize(tokens.astype(jnp.float32)).astype(jnp.bfloat16)
        gathers.append([net.start(normed.at[kept], normed.at[kept], peers[k - 1]) for k in (1, 3)])
        if chunk == CHUNKS - 1:
            gathers[0][0].wait_recv()
            passed = [hand_on(normed, neighbour(-1, 0, CHUNK), 0)]
        serve(f"swap{chunk}")
    gathers[1][1].wait_recv()
    passed.append(hand_on(normed, neighbour(1, CHUNK, CHUNK), 1))
    gathers[2][0].wait_recv()
    passed.append(hand_on(normed, neighbour(-1, 2 * CHUNK, CHUNK // 2), 0))
    gathers[2][1].wait_recv()
    passed.append(hand_on(normed, neighbour(1, 2 * CHUNK + CHUNK // 2, CHUNK // 2), 1))
    gathers[0][1].wait_recv()
    gathers[1][0].wait_recv()
    for copy in passed:
        copy.wait_recv()
    for copy in qkv_copies:
        copy.wait()
    serve("ag1")
    @pl.loop(0, HEADS // 2)
    def _(pair):
        columns = pl.ds(pl.multiple_of(pair * 256, 256), 256)
        rows = normed[...]
        q = dot(rows, qkv_w[0, :, columns])
        k = dot(rows, qkv_w[1, :, columns])
        v = dot(rows, qkv_w[2, :, columns])
        value[:, columns] = v.astype(jnp.bfloat16)
        for side in range(2):
            part = slice(side * HEAD_DIM, (side + 1) * HEAD_DIM)
            lanes = pl.ds(pl.multiple_of(pair * 256 + side * HEAD_DIM, HEAD_DIM), HEAD_DIM)
            turned = k[:, part] * cosine[...] + pltpu.roll(k[:, part], HEAD_DIM // 2, 1) * sine[...]
            key[:, lanes] = turned.astype(jnp.bfloat16)
            turned = q[:, part] * cosine[...] + pltpu.roll(q[:, part], HEAD_DIM // 2, 1) * sine[...]
            turned = turned.astype(jnp.bfloat16)
            for half, m in blocks:
                query[kept_at(half, m), lanes] = turned[token_at(half, m)]

    serve("qkv")
    for copy in cache_copies[:-2]:
        copy.wait_recv()
    for copy in cache_copies[-2:]:
        copy.wait()
    o_copy.wait()

    scale = 1.0 / math.sqrt(HEAD_DIM)
    own_part = [
        pl.ds(pl.multiple_of(half * HALF + mp * PART, PART), PART) for half in range(2)
    ]

    def attend(half):
        @pl.loop(0, HEADS)
        def _(h):
            columns = pl.ds(pl.multiple_of(h * HEAD_DIM, HEAD_DIM), HEAD_DIM)
            inner = (((1,), (1,)), ((), ()))
            for block in range(2):
                rows = slice(half * HALF + block * 96, half * HALF + block * 96 + 96)
                q = query[rows, columns]
                old = dot(q, cache[0, :, columns], inner) * scale + bias[rows, :CACHE]
                new = dot(q, key[:, columns], inner) * scale + bias[rows, CACHE:]
                top = jnp.maximum(
                    jnp.max(old, axis=1, keepdims=True), jnp.max(new, axis=1, keepdims=True)
                )
                old, new = jnp.exp(old - top), jnp.exp(new - top)
                total = jnp.sum(old, axis=1, keepdims=True) + jnp.sum(new, axis=1, keepdims=True)
                share = 1.0 / total
                out = dot((old * share).astype(jnp.bfloat16), cache[1, :, columns])
                out = out + dot((new * share).astype(jnp.bfloat16), value[:, columns])
                mixed[rows, columns] = out.astype(jnp.bfloat16)

    def scatter(half, columns, send, recv):
        copies = []
        for k in (2, 1, 3):
            rows = pl.ds(pl.multiple_of(half * HALF + lax.rem(mp + k, 4) * PART, PART), PART)
            copies.append(
                net.start(
                    send.at[rows, columns],
                    recv.at[k - 1, half * PART : (half + 1) * PART, columns],
                    peers[k - 1],
                )
            )
        return copies

    def collect(half, columns, copies, recv):
        for copy in copies:
            copy.wait_recv()
        total = terms[own_part[half], columns]
        for k in range(3):
            total = total + recv[k, half * PART : (half + 1) * PART, columns].astype(jnp.float32)
        return total

    def project(half):
        rows = slice(half * HALF, (half + 1) * HALF)
        for tile in range(4):
            columns = slice(tile * 512, (tile + 1) * 512)
            part = dot(mixed[rows, :], o_w[:, columns])
            terms[rows, columns] = part
            send_one[rows, columns] = part.astype(jnp.bfloat16)
        return scatter(half, slice(0, D), send_one, recv_one)

    scattered = []
    for half in range(2):
        attend(half)
        scattered.append(project(half))
        serve(f"attn{half}")


    gathers = []
    for half in range(2):
        rows = slice(half * PART, (half + 1) * PART)
        own = jnp.where(moved, other_tokens[rows, :], tokens_ref[rows, :])
        total = collect(half, slice(0, D), scattered[half], recv_one)
        fresh = (own.astype(jnp.float32) + total).astype(jnp.bfloat16)
        state[rows, :] = fresh
        kept = own_part[half]
        normed_two[kept, :] = normalize(fresh.astype(jnp.float32)).astype(jnp.bfloat16)
        gathers.append(
            [net.start(normed_two.at[kept], normed_two.at[kept], peers[k - 1]) for k in (1, 3)]
        )
        if half == 0:
            serve("rs0")

    for half, off in enumerate((-1, 1)):
        gathers[half].pop(half).wait_recv()
        theirs = pl.ds(
            pl.multiple_of(half * HALF + lax.rem(mp + off + 4, 4) * PART, PART), PART
        )
        gathers[half].append(hand_on(normed_two, theirs, half))
    serve("rs1")
    sib_own.wait_recv()
    serve("ag2")
    def raise_up(half):
        for copy in gathers[half]:
            copy.wait_recv()

        @pl.loop(0, FF // 512)
        def _(tile):
            columns = pl.ds(pl.multiple_of(tile * 512, 512), 512)
            rows = normed_two[half * HALF : (half + 1) * HALF, :]
            gate = dot(rows, w[0, :, :, :, :, columns].reshape(D, 512))
            upward = dot(rows, w[1, :, :, :, :, columns].reshape(D, 512))
            hidden[half * HALF : (half + 1) * HALF, columns] = (
                gate / (1.0 + jnp.exp(-gate)) * upward
            ).astype(jnp.bfloat16)

    raise_up(0)
    serve("up0")
    raise_up(1)
    serve("up1")
    units = [(tile, half) for tile in range(4) for half in range(2)]
    scattered = []
    returns = []

    def features(tile):
        at = lax.rem(x + (0, -1, 1, 2)[tile] + 4, 4)
        return [pl.ds(pl.multiple_of(zone * 512 + at * 128, 128), 128) for zone in range(4)]

    def give_back(unit):
        tile, half = units[unit]
        rows = slice(half * PART, (half + 1) * PART)
        for copy in scattered[unit]:
            copy.wait_recv()
        total = sums[tile, own_part[half]]
        for k in range(3):
            total = total + recv_two[k, tile, rows].astype(jnp.float32)
        base = jnp.concatenate([state[rows, lanes] for lanes in features(tile)], axis=1)
        done[tile, rows] = (base.astype(jnp.float32) + total).astype(jnp.bfloat16)
        part = net.start(done.at[tile, rows], other_done.at[tile, rows], partner)
        returns.append((tile, rows, part))

    serve("tile0")
    for unit, (tile, half) in enumerate(units):
        if half == 0 and tile in (1, 3):
            serve(f"tile{tile}")
        at = lax.rem(x + (0, -1, 1, 2)[tile] + 4, 4)
        rows = slice(half * HALF, (half + 1) * HALF)
        matrix = w[2, :, at].reshape(TILE, FF)
        part = dot(hidden[rows, :], matrix, (((1,), (1,)), ((), ())))
        sums[tile, rows] = part
        send_two[tile, rows] = part.astype(jnp.bfloat16)
        copies = []
        for k in (2, 1, 3):
            theirs = pl.ds(
                pl.multiple_of(half * HALF + lax.rem(mp + k, 4) * PART, PART), PART
            )
            target = recv_two.at[k - 1, tile, half * PART : (half + 1) * PART]
            copies.append(net.start(send_two.at[tile, theirs], target, peers[k - 1]))
        scattered.append(copies)
        if unit >= LAG:
            give_back(unit - LAG)
    for unit in range(len(units) - LAG, len(units)):
        give_back(unit)
    for tile, rows, part in returns:
        part.wait_recv()
        chosen = jnp.where(moved, other_done[tile, rows], done[tile, rows])
        for zone, lanes in enumerate(features(tile)):
            out_ref[rows, lanes] = chosen[:, zone * 128 : (zone + 1) * 128]
    for copy in net.all:
        if all(copy is not gone for gone in net.gone):
            copy.wait_send()


N_COPIES = 12 + 3 * CHUNKS + N_STREAM_COPIES * 3 + 12 + 32 + CHUNKS


def local(
    tokens,
    request_ids,
    cache_entries,
    cached_lengths,
    traded,
    query_weight,
    key_weight,
    value_weight,
    output_weight,
    gate_weight,
    up_weight,
    down_weight,
):
    half = HEAD_DIM // 2
    freq = ROPE_BASE ** (-np.arange(half, dtype=np.float64) / half)
    freq = jnp.asarray(np.concatenate([freq, freq])[None].astype(np.float32))
    bf16, f32 = jnp.bfloat16, jnp.float32
    in_vmem = pl.BlockSpec(memory_space=pltpu.VMEM)
    in_smem = pl.BlockSpec(memory_space=pltpu.SMEM)
    in_hbm = pl.BlockSpec(memory_space=pl.ANY)
    return pl.pallas_call(
        kernel,
        out_shape=jax.ShapeDtypeStruct((OWN, D), bf16),
        in_specs=[in_smem, in_smem, in_vmem, in_vmem, in_vmem] + [in_hbm] * 8,
        out_specs=in_vmem,
        scratch_shapes=[
            pltpu.VMEM((3, 4, 4, 2, 64, D), bf16),
            pltpu.VMEM((3, D, WIDTH), bf16),
            pltpu.VMEM((WIDTH, D), bf16),
            pltpu.VMEM((2, CACHE, WIDTH), bf16),
            pltpu.VMEM((OWN, D), bf16),
            pltpu.VMEM((1, GROUP), jnp.int32),
            pltpu.VMEM((GROUP, D), bf16),
            pltpu.VMEM((GROUP, WIDTH), bf16),
            pltpu.VMEM((GROUP, WIDTH), bf16),
            pltpu.VMEM((GROUP, WIDTH), bf16),
            pltpu.VMEM((GROUP, HEAD_DIM), f32),
            pltpu.VMEM((GROUP, HEAD_DIM), f32),
            pltpu.VMEM((GROUP, CACHE + GROUP), f32),
            pltpu.VMEM((GROUP, WIDTH), bf16),
            pltpu.VMEM((GROUP, D), f32),
            pltpu.VMEM((GROUP, D), bf16),
            pltpu.VMEM((3, OWN, D), bf16),
            pltpu.VMEM((OWN, D), bf16),
            pltpu.VMEM((GROUP, D), bf16),
            pltpu.VMEM((GROUP, FF), bf16),
            pltpu.VMEM((4, GROUP, TILE), f32),
            pltpu.VMEM((4, GROUP, TILE), bf16),
            pltpu.VMEM((3, 4, OWN, TILE), bf16),
            pltpu.VMEM((4, OWN, TILE), bf16),
            pltpu.VMEM((4, OWN, TILE), bf16),
            pltpu.SemaphoreType.DMA((N_COPIES,)),
            pltpu.SemaphoreType.DMA((N_COPIES,)),
            pltpu.SemaphoreType.DMA((9,)),
        ],
        compiler_params=pltpu.CompilerParams(
            collective_id=0, has_side_effects=True, vmem_limit_bytes=60 * 1024 * 1024
        ),
        name="layer",
    )(
        traded,
        cached_lengths.T,
        tokens,
        request_ids,
        freq,
        cache_entries,
        query_weight,
        key_weight,
        value_weight,
        output_weight,
        gate_weight,
        up_weight,
        down_weight,
    )


def solution(mesh):
    in_specs = (
        P(("rep", "dp", "mp"), None),
        P(("rep", "dp"), None),
        P(("rep", "dp", "mp"), None),
        P(),
        P("dp"),
        P(None, "mp"),
        P(None, "mp"),
        P(None, "mp"),
        P("mp", None),
        P("dp", "mp"),
        P("dp", "mp"),
        P("dp", "mp"),
    )
    out_specs = P(("rep", "dp", "mp"), None)
    return jax.shard_map(local, mesh=mesh, in_specs=in_specs, out_specs=out_specs, check_vma=False)
```
